128 devices in a mesh: radar: 8 (over x, core), tile: 16 (over y, z).
Axes of the slice: x: 4, y: 4, z: 4, core: 2. Of those that a mesh axis runs over, the one named last changes fastest.
Arguments:
- background: float32 [3, 256, 32, 2048], P(None, 'tile', None, 'radar'), may hold values from -6 to 6
- interp: bfloat16 [32768, 128, 128], P(('radar', 'tile')), may hold values from -0.5 to 0.5
- beam: bfloat16 [32768, 3, 128], P(('radar', 'tile')), may hold values from -1 to 1
- observed: bfloat16 [32768, 128], P(('radar', 'tile')), may hold values from -6 to 6
- cell_block: int32 [32768], P(('radar', 'tile')), may hold values from 0 to 1023
- sweep_count: int32 [128, 128], P(('radar', 'tile')), may hold values from 0 to 2, as said below
Outputs:
- wind_field: float32 [3, 256, 32, 2048], P(None, 'tile', None, 'radar')
- strain: float32 [6, 256, 32, 2048], P(None, 'tile', None, 'radar')
- cost_trace: float32 [2], replicated
The draws below stay inside these ranges and needn't reach their ends.
Inputs may be any that keep to these rules, and one draw needn't show every extreme that they name: `cell_block`: the cell block, within the owner's 16 x 32 x 256 cells of one component, read by a slot. `sweep_count`: every source device has an owning device to which all 2 of its slots are live.
All inputs are finite; a program needn't handle non-finite values.
Results may differ from the reference program's by a relative error of at most 0.0014.
Values may be sent and summed in bfloat16 or wider, within the bound.
A program may use at most 64 MiB of HBM per device.

```python
import jax
import jax.numpy as jnp
from jax import lax

CX = 16
CY = 256
NZ = 32
GATE = 128
CAP = 2
ITERS = 2
NDEV = 128
BLOCKS = 32768
NX = 256
NY = 2048
N_RADAR = 8
N_TILE = 16


def draw_sweep_count(key, part):
    first_key, second_key = jax.random.split(jax.random.fold_in(key, 11))
    counts = jax.random.randint(first_key, (NDEV, NDEV), 0, CAP + 1)
    full_owner = jax.random.randint(second_key, (NDEV,), 0, NDEV)
    chosen = jnp.arange(NDEV)[None, :] == full_owner[:, None]
    return jnp.where(chosen, CAP, counts).astype(jnp.int32)


def set_ends(entries, rng, smallest, largest):
    longest = entries.shape.index(max(entries.shape))
    spots = []
    for shift in (0, 1):
        where = [jax.random.randint(jax.random.fold_in(rng, axis), (), 0, length) for axis, length in enumerate(entries.shape)]
        where[longest] = (where[longest] + shift) % entries.shape[longest]
        spots.append(tuple(where))
    return entries.at[spots[0]].set(smallest).at[spots[1]].set(largest)


def levels(own_key, dims, cuts, low, largest):
    loudness, own = 1.0, jax.random.fold_in(own_key, 6)
    for axis_at, parts in cuts:
        steps = jnp.exp(jax.random.uniform(jax.random.fold_in(own, axis_at), (parts,), jnp.float32, low / len(cuts), largest / len(cuts)))
        loudness = loudness * jnp.repeat(steps, dims[axis_at] // parts).reshape([-1 if axis == axis_at else 1 for axis in range(len(dims))])
    return loudness


def normal_values(own_key, dims, width, bound, shards=(), held_as=jnp.bfloat16):
    values = jax.random.normal(own_key, dims, jnp.float32) * width
    if len(shards) > 0:
        values = levels(own_key, dims, shards, -0.22, 0.18) * values
    return jnp.clip(values, min=-bound, max=bound).astype(held_as)


def setup_inputs(seed: int = 0) -> dict:
    streams_of = jax.random.split(jax.random.key(seed), 7)
    return {
        "background": normal_values(streams_of[0], (3, NX, NZ, NY), 1.0, 6.0, ((1, 16), (3, 8)), jnp.float32),
        "interp": normal_values(streams_of[1], (BLOCKS, GATE, GATE), GATE ** -0.5, 0.5, ((0, 128),)),
        "beam": jnp.clip(jax.random.uniform(streams_of[2], (BLOCKS, 3, GATE), jnp.float32, -1.0, 1.0) * levels(streams_of[2], (BLOCKS, 3, GATE), ((0, 128),), -0.4, 0.0), -1.0, 1.0).astype(jnp.bfloat16),
        "observed": normal_values(streams_of[3], (BLOCKS, GATE), 1.0, 6.0, ((0, 128),)),
        "cell_block": set_ends(jax.random.randint(streams_of[4], (BLOCKS,), 0, CX * NZ * CY // GATE), jax.random.fold_in(streams_of[4], 1), 0, (CX * NZ * CY // GATE) - 1).astype(jnp.int32),
        "sweep_count": draw_sweep_count(jax.random.fold_in(streams_of[6], 71), 0),
    }


BACKGROUND_WEIGHT = 0.5
DIVERGENCE_WEIGHT = 1.0
STEP_LENGTH = 0.3
EPSILON = 1e-06

def central(values, which_axis):
    extent = values.shape[which_axis]
    widths = [(0, 0)] * values.ndim
    widths[which_axis] = (1, 1)
    padded = jnp.pad(values, widths)
    upper_part = lax.slice_in_dim(padded, 2, extent + 2, axis=which_axis)
    lower_part = lax.slice_in_dim(padded, 0, extent, axis=which_axis)
    return 0.5 * (upper_part - lower_part)

def to_blocks(grid_field):
    blocked = grid_field.reshape(3, N_TILE, CX, NZ, N_RADAR, CY // GATE, GATE)
    blocked = blocked.transpose(4, 1, 0, 2, 3, 5, 6)
    return blocked.reshape(N_RADAR * N_TILE, 3, CX * NZ * (CY // GATE), GATE)

def from_blocks(blocked):
    shaped = blocked.reshape(N_RADAR, N_TILE, 3, CX, NZ, CY // GATE, GATE)
    shaped = shaped.transpose(2, 1, 3, 4, 0, 5, 6)
    return shaped.reshape(3, N_TILE * CX, NZ, N_RADAR * CY)

def observation_term(wind_field, interp, beam, observed, cell_block, sweep_count):
    devices = N_RADAR * N_TILE
    blocked = to_blocks(wind_field).astype(jnp.bfloat16)
    weights = interp.reshape(devices, devices, CAP, GATE, GATE)
    beam_rows = beam.reshape(devices, devices, CAP, 3, GATE)
    looked = observed.reshape(devices, devices, CAP, GATE)
    indices = cell_block.reshape(devices, devices, CAP).astype(jnp.int32)
    alive_mask = (jnp.arange(CAP, dtype=jnp.int32)[None, None, :] < sweep_count[:, :, None]).astype(jnp.float32)
    owners = jnp.arange(devices, dtype=jnp.int32)[:, None]

    def one_source(pieces):
        weight_src, beam_src, looked_src, index_src, alive_src = pieces
        cell_rows = lax.optimization_barrier(blocked[owners, :, index_src])
        weight_full = weight_src.astype(jnp.float32)
        projected = jnp.einsum('dskc,dsgc->dskg', cell_rows.astype(jnp.float32), weight_full)
        beam_values = beam_src.astype(jnp.float32)
        radial = lax.optimization_barrier(jnp.sum(beam_values * projected, axis=2))
        misfit = alive_src[..., None] * (radial - looked_src.astype(jnp.float32))
        adjoint = lax.optimization_barrier((beam_values * misfit[:, :, None, :]).astype(jnp.bfloat16))
        returned = jnp.einsum('dskg,dsgc->dskc', adjoint.astype(jnp.float32), weight_full)
        return (0.5 * jnp.sum(misfit * misfit), returned)
    misfit_cost, returned_all = lax.map(one_source, (weights, beam_rows, looked, indices, alive_mask))
    owner_index = jnp.broadcast_to(owners[None, :, :], indices.shape)
    gradient = jnp.zeros((devices, 3, CX * NZ * (CY // GATE), GATE), jnp.float32)
    gradient = gradient.at[owner_index, :, indices].add(returned_all)
    return (jnp.sum(misfit_cost), from_blocks(gradient))

def reference(background, interp, beam, observed, cell_block, sweep_count):
    wind_field = background
    trace = []
    for step_index in range(ITERS):
        obs_cost, obs_grad = observation_term(wind_field, interp, beam, observed, cell_block, sweep_count)
        spread = central(wind_field[0], 0) + central(wind_field[1], 2) + central(wind_field[2], 1)
        offset = wind_field - background
        push = jnp.stack([-central(spread, 0), -central(spread, 2), -central(spread, 1)])
        gradient = obs_grad + BACKGROUND_WEIGHT * offset + DIVERGENCE_WEIGHT * push
        total_cost = obs_cost + 0.5 * BACKGROUND_WEIGHT * jnp.sum(offset * offset) + 0.5 * DIVERGENCE_WEIGHT * jnp.sum(spread * spread)
        scale = jnp.sqrt(jnp.sum(gradient * gradient) / gradient.size + EPSILON)
        wind_field = wind_field - STEP_LENGTH * gradient / scale
        trace.append(total_cost / (N_RADAR * N_TILE * N_RADAR * N_TILE * CAP * GATE))
    east_wind, north_wind, upward_wind = (wind_field[0], wind_field[1], wind_field[2])
    strain = jnp.stack([central(east_wind, 0), central(north_wind, 2), central(upward_wind, 1), 0.5 * (central(east_wind, 2) + central(north_wind, 0)), 0.5 * (central(east_wind, 1) + central(upward_wind, 0)), 0.5 * (central(north_wind, 1) + central(upward_wind, 2))])
    return (wind_field, strain, jnp.stack(trace))
```

```python
import functools

import jax
import jax.numpy as jnp
from jax import lax
from jax.experimental import pallas as pl
from jax.experimental.pallas import tpu as pltpu
from jax.sharding import PartitionSpec as P

BACKGROUND_WEIGHT = 0.5
DIVERGENCE_WEIGHT = 1.0
STEP_LENGTH = 0.3
EPSILON = 1e-06
GROUP = 8
LANES = 128
F32 = jnp.float32
BF16 = jnp.bfloat16
LOGICAL = pl.DeviceIdType.LOGICAL
BACK, SPREAD0, GRAD0, SPREAD1, GRAD1 = range(5)


def iota(shape, dim):
    return lax.broadcasted_iota(jnp.int32, shape, dim)


def kernel(sizes, bg_hbm, interp_hbm, codes_ref, beam_ref, looked_ref,
           wind_ref, strain_ref, cost_ref,
           weights, wind, grad0, grad1, spread0, spread1, push,
           codes_in, out1, in1, out2, in2, out3, in3, out4, in4, out5, in5,
           pick, place, field, misfit0, edges_out, edges_in,
           send_sems, recv_sems, halo_send, halo_recv, local_sems):
    n_radar, n_tile, total_cells, total_gates = sizes
    n = n_radar * n_tile
    nx, nz, ny = wind.shape[1] - 2, wind.shape[2], wind.shape[3]
    half = nx * nz
    r, t = lax.axis_index("radar"), lax.axis_index("tile")
    me = r * n_tile + t
    other = jnp.where(me + 1 >= n, me + 1 - n, me + 1)

    load_bg = pltpu.make_async_copy(bg_hbm, wind.at[:, pl.ds(1, nx)], local_sems.at[0])
    load_interp = pltpu.make_async_copy(interp_hbm, weights, local_sems.at[1])
    load_bg.start()
    load_interp.start()

    barrier = pltpu.get_barrier_semaphore()

    def greet(k, carry):
        d = me + k
        d = jnp.where(d >= n, d - n, d)
        pl.semaphore_signal(barrier, inc=1, device_id=d, device_id_type=LOGICAL)
        return carry

    lax.fori_loop(1, n, greet, 0)

    lane = iota((nz, LANES), 1)

    def pack_edges(stage, source, comps, one_field):
        def plane(x, carry):
            low, high = carry
            for k in range(comps):
                if one_field:
                    a, b = source[x + 1, :, :LANES], source[x + 1, :, ny - LANES :]
                else:
                    a, b = source[k, x + 1, :, :LANES], source[k, x + 1, :, ny - LANES :]
                to = 8 * x + k
                a = pltpu.roll(a, to, 1)
                b = pltpu.roll(b, to + 1, 1)
                low = jnp.where(lane == to, a, low)
                high = jnp.where(lane == to, b, high)
            return low, high

        zero = jnp.zeros((nz, LANES), F32)
        low, high = lax.fori_loop(0, nx, plane, (zero, zero))
        edges_out[stage, 0] = low
        edges_out[stage, 1] = high

    def halo_copies(stage, array, one_field):
        def planes(x):
            return array.at[x] if one_field else array.at[:, x]

        def make(i, src, dst, device):
            return pltpu.make_async_remote_copy(
                src_ref=src, dst_ref=dst,
                send_sem=halo_send.at[stage, i], recv_sem=halo_recv.at[stage, i],
                device_id=device, device_id_type=LOGICAL)

        up_t = jnp.where(t < n_tile - 1, me + 1, me - 1)
        down_t = jnp.where(t > 0, me - 1, me + 1)
        up_r = jnp.where(r < n_radar - 1, me + n_tile, me - n_tile)
        down_r = jnp.where(r > 0, me - n_tile, me + n_tile)
        return (
            (t < n_tile - 1, t > 0, make(0, planes(nx), planes(0), up_t)),
            (t > 0, t < n_tile - 1, make(1, planes(1), planes(nx + 1), down_t)),
            (r < n_radar - 1, r > 0, make(2, edges_out.at[stage, 1], edges_in.at[stage, 0], up_r)),
            (r > 0, r < n_radar - 1, make(3, edges_out.at[stage, 0], edges_in.at[stage, 1], down_r)),
        )

    def send_halos(stage, array, one_field=False):
        for i, (sends, receives, copy) in enumerate(halo_copies(stage, array, one_field)):
            pl.when(sends)(copy.start)

            @pl.when(jnp.logical_not(receives))
            def _():
                if i >= 2:
                    edges_in[stage, i - 2] = jnp.zeros((nz, LANES), F32)
                elif one_field:
                    array[(nx + 1) * i] = jnp.zeros((nz, ny), F32)
                else:
                    array[:, (nx + 1) * i] = jnp.zeros((3, nz, ny), F32)

    def await_halos(stage, array, one_field=False):
        for sends, receives, copy in halo_copies(stage, array, one_field):
            pl.when(sends)(copy.wait_send)
            pl.when(receives)(copy.wait_recv)

    def exchange_copy(stage, src, dst, d):
        return pltpu.make_async_remote_copy(
            src_ref=src.at[d], dst_ref=dst.at[me],
            send_sem=send_sems.at[stage], recv_sem=recv_sems.at[stage],
            device_id=d, device_id_type=LOGICAL)

    def send_all(stage, src, dst):
        def one(k, carry):
            d = me + k
            d = jnp.where(d >= n, d - n, d)
            exchange_copy(stage, src, dst, d).start()
            return carry

        lax.fori_loop(1, n, one, 0)
        dst[me] = src[me]

    def whole(stage, src, dst):
        return pltpu.make_async_remote_copy(
            src_ref=src.at[pl.ds(0, n - 1)], dst_ref=dst.at[pl.ds(0, n - 1)],
            send_sem=send_sems.at[stage], recv_sem=recv_sems.at[stage],
            device_id=other, device_id_type=LOGICAL)

    sub = iota((nz, ny), 0)
    wide = iota((nz, ny), 1)

    def diff_z(v):
        up = jnp.where(sub == nz - 1, 0.0, pltpu.roll(v, nz - 1, 0))
        down = jnp.where(sub == 0, 0.0, pltpu.roll(v, 1, 0))
        return 0.5 * (up - down)

    def diff_y(v, low, high, x, k):
        at = 8 * x + k
        low = pltpu.roll(low, lax.rem(LANES - at, LANES), 1)
        high = pltpu.roll(high, LANES - 1 - at, 1)
        up = jnp.where(wide == ny - 1, jnp.concatenate([high] * (ny // LANES), 1), pltpu.roll(v, ny - 1, 1))
        down = jnp.where(wide == 0, jnp.concatenate([low] * (ny // LANES), 1), pltpu.roll(v, 1, 1))
        return 0.5 * (up - down)

    def divergence(stage, source, out):
        low, high = edges_in[stage, 0], edges_in[stage, 1]

        def plane(x, total):
            s = (0.5 * (source[0, x + 2] - source[0, x]) + diff_y(source[1, x + 1], low, high, x, 1)
                 + diff_z(source[2, x + 1]))
            out[x + 1] = s
            return total + s * s

        return lax.fori_loop(0, nx, plane, jnp.zeros((nz, ny), F32))

    def pushes(stage, source, x, low, high):
        v = source[x + 1]
        return (0.5 * (source[x] - source[x + 2]), -diff_y(v, low, high, x, 0), -diff_z(v))

    def total_of(v):
        return jnp.sum(jnp.sum(v, axis=0, keepdims=True), axis=1, keepdims=True)

    def to_field(source):
        for h in range(ny // LANES):
            for k in range(3):
                v = source[k, 1 : nx + 1, :, h * LANES : (h + 1) * LANES]
                field[h * half : (h + 1) * half, k * LANES : (k + 1) * LANES] = v.reshape(half, LANES).astype(BF16)

    def gather(out, extra):
        chosen = jnp.dot(pick[...], field[...], preferred_element_type=F32)
        zero = jnp.zeros((n, LANES), F32)
        rows = []
        for k in range(2):
            for c in range(3):
                rows.append(chosen[k * n : (k + 1) * n, c * LANES : (c + 1) * LANES])
            rows.append(zero if k == 1 or extra is None else jnp.broadcast_to(extra, (n, LANES)))
        out[...] = jnp.swapaxes(jnp.stack(rows, 0), 0, 1).astype(BF16)

    def observe(source, out, dst, stage, step):
        def some(g, cost):
            for u in range(GROUP):
                d = g * GROUP + u
                both = weights[pl.ds(2 * d, 2)].reshape(2 * LANES, LANES)
                projected = lax.dot_general(source[d], both, (((1,), (1,)), ((), ())), preferred_element_type=F32)
                beams = beam_ref[d]
                radial = jnp.sum(beams * projected, axis=0, keepdims=True)
                if step is None:
                    misfit = radial - looked_ref[d]
                    misfit0[d] = misfit
                else:
                    misfit = misfit0[d] - step * radial
                cost = cost + misfit * misfit
                adjoint = (beams * misfit).astype(BF16)
                out[d] = jnp.dot(adjoint, both, preferred_element_type=F32).astype(BF16)
            return cost

        cost = lax.fori_loop(0, n // GROUP, some, jnp.zeros((1, 2 * LANES), F32))
        send_all(stage, out, dst)
        return 0.5 * jnp.sum(cost, axis=1, keepdims=True)

    def scatter(source, out):
        rows = jnp.swapaxes(source[...].astype(F32), 0, 1).astype(BF16)
        landed = jnp.concatenate(
            [jnp.concatenate([rows[4 * k + c] for c in range(3)], 1) for k in range(2)], 0)
        for h in range(ny // LANES):
            added = jnp.dot(place[h * half : (h + 1) * half], landed, preferred_element_type=F32)
            for c in range(3):
                lanes = slice(h * LANES, (h + 1) * LANES)
                v = added[:, c * LANES : (c + 1) * LANES].reshape(nx, nz, LANES)
                out[c, 1 : nx + 1, :, lanes] = v + push[c, :, :, lanes]

    def square_sum(source):
        def plane(x, total):
            for c in range(3):
                v = source[c, x + 1]
                total = total + v * v
            return total

        return total_of(lax.fori_loop(0, nx, plane, jnp.zeros((nz, ny), F32)))

    load_bg.wait()
    pack_edges(BACK, wind, 3, False)
    pl.semaphore_wait(barrier, n - 1)

    send_all(0, codes_ref, codes_in)
    send_halos(BACK, wind)
    to_field(wind)
    whole(0, codes_ref, codes_in).wait_recv()
    rows = jnp.swapaxes(codes_in[...].astype(F32), 0, 1)
    for k in range(2):
        code = (rows[4 * k] * LANES + rows[4 * k + 1]).astype(jnp.int32)
        across = jnp.transpose(code)
        for j in range(pick.shape[1] // LANES):
            hit = code == iota((n, LANES), 1) + j * LANES
            pick[k * n : (k + 1) * n, j * LANES : (j + 1) * LANES] = jnp.where(hit, 1.0, 0.0).astype(BF16)
            hit = across == iota((LANES, n), 0) + j * LANES
            place[j * LANES : (j + 1) * LANES, k * n : (k + 1) * n] = jnp.where(hit, 1.0, 0.0).astype(BF16)

    gather(out1, None)
    send_all(1, out1, in1)
    await_halos(BACK, wind)
    spread_cost0 = 0.5 * DIVERGENCE_WEIGHT * total_of(divergence(BACK, wind, spread0))
    pack_edges(SPREAD0, spread0, 1, True)
    send_halos(SPREAD0, spread0, True)
    load_interp.wait()
    whole(1, out1, in1).wait_recv()
    cost0 = observe(in1, out2, in2, 2, None) + spread_cost0
    await_halos(SPREAD0, spread0, True)
    low, high = edges_in[SPREAD0, 0], edges_in[SPREAD0, 1]

    def push_plane(x, carry):
        for c, v in enumerate(pushes(SPREAD0, spread0, x, low, high)):
            push[c, x] = DIVERGENCE_WEIGHT * v
        return carry

    lax.fori_loop(0, nx, push_plane, 0)
    whole(2, out2, in2).wait_recv()
    scatter(in2, grad0)
    squares = square_sum(grad0)
    to_field(grad0)

    first = squares.astype(BF16)
    rest = squares - first.astype(F32)
    second = rest.astype(BF16)
    third = (rest - second.astype(F32)).astype(BF16)
    at = iota((1, LANES), 1)
    extra = jnp.where(at == 0, first.astype(F32), jnp.where(at == 1, second.astype(F32), jnp.where(at == 2, third.astype(F32), 0.0)))
    gather(out3, extra)
    send_all(3, out3, in3)
    pack_edges(GRAD0, grad0, 3, False)
    send_halos(GRAD0, grad0)
    await_halos(GRAD0, grad0)
    divergence(GRAD0, grad0, spread1)
    pack_edges(SPREAD1, spread1, 1, True)
    send_halos(SPREAD1, spread1, True)
    whole(3, out3, in3).wait_recv()
    squares = jnp.sum(jnp.sum(in3[...].astype(F32), axis=0)[3:4], axis=1, keepdims=True)
    step0 = STEP_LENGTH / jnp.sqrt(squares / total_cells + EPSILON)
    cost1 = observe(in3, out4, in4, 4, step0)
    await_halos(SPREAD1, spread1, True)
    low1, high1 = edges_in[SPREAD1, 0], edges_in[SPREAD1, 1]

    def update_plane(x, carry):
        offsets, spreads = carry
        for c, v in enumerate(pushes(SPREAD1, spread1, x, low1, high1)):
            offset = -step0 * grad0[c, x + 1]
            offsets = offsets + offset * offset
            push[c, x] = push[c, x] - step0 * (DIVERGENCE_WEIGHT * v) + BACKGROUND_WEIGHT * offset
        spread = spread0[x + 1] - step0 * spread1[x + 1]
        return offsets, spreads + spread * spread

    zero = jnp.zeros((nz, ny), F32)
    offsets, spreads = lax.fori_loop(0, nx, update_plane, (zero, zero))
    cost1 = cost1 + 0.5 * total_of(BACKGROUND_WEIGHT * offsets + DIVERGENCE_WEIGHT * spreads)

    def wind_plane(x, carry):
        for c in range(3):
            wind[c, x] = wind[c, x] - step0 * grad0[c, x]
        return carry

    lax.fori_loop(0, nx + 2, wind_plane, 0)
    whole(4, out4, in4).wait_recv()
    scatter(in4, grad1)

    pack_edges(GRAD1, grad1, 3, False)
    send_halos(GRAD1, grad1)
    squares = square_sum(grad1)
    summary = jnp.where(at == 0, squares, jnp.where(at == 1, cost0, jnp.where(at == 2, cost1, 0.0)))

    def fill(d, carry):
        out5[d] = summary
        return carry

    lax.fori_loop(0, n, fill, 0)
    send_all(5, out5, in5)
    whole(5, out5, in5).wait_recv()
    sums = jnp.sum(in5[...], axis=0)
    cost_ref[...] = sums / total_gates
    squares = jnp.sum(jnp.where(at == 0, sums, 0.0), axis=1, keepdims=True)
    step1 = STEP_LENGTH / jnp.sqrt(squares / total_cells + EPSILON)
    await_halos(GRAD1, grad1)

    def last_plane(x, carry):
        for c in range(3):
            wind[c, x] = wind[c, x] - step1 * grad1[c, x]
        return carry

    lax.fori_loop(0, nx + 2, last_plane, 0)
    low, high = (edges_in[BACK, i] - step0 * edges_in[GRAD0, i] - step1 * edges_in[GRAD1, i] for i in range(2))

    def strain_plane(x, carry):
        v = [wind[c, x + 1] for c in range(3)]
        dx = [0.5 * (wind[c, x + 2] - wind[c, x]) for c in range(3)]
        dy = [diff_y(v[c], low, high, x, c) for c in range(3)]
        dz = [diff_z(v[c]) for c in range(3)]
        for c in range(3):
            wind_ref[c, x] = v[c]
        strain_ref[0, x] = dx[0]
        strain_ref[1, x] = dy[1]
        strain_ref[2, x] = dz[2]
        strain_ref[3, x] = 0.5 * (dy[0] + dx[1])
        strain_ref[4, x] = 0.5 * (dz[0] + dx[2])
        strain_ref[5, x] = 0.5 * (dz[1] + dy[2])
        return carry

    lax.fori_loop(0, nx, strain_plane, 0)

    pairs = ((codes_ref, codes_in), (out1, in1), (out2, in2), (out3, in3), (out4, in4), (out5, in5))
    for stage, (src, dst) in enumerate(pairs):
        whole(stage, src, dst).wait_send()


def shards(n_radar, n_tile, background, interp, beam, observed, cell_block, sweep_count):
    n = n_radar * n_tile
    _, nx, nz, ny = background.shape
    slots = interp.shape[0] // n
    gate = interp.shape[1]
    blocks = nx * nz * ny // gate
    total_cells = 3 * nx * nz * ny * n
    total_gates = interp.shape[0] * n * gate
    sizes = (n_radar, n_tile, total_cells, total_gates)
    across = ny // gate

    alive = jnp.arange(slots, dtype=jnp.int32)[None, :] < sweep_count.reshape(n)[:, None]
    index = cell_block.reshape(n, slots)
    code = (index % across) * (blocks // across) + index // across
    top = jnp.where(alive, code // LANES, -1)
    low = jnp.where(alive, code % LANES, 0)
    nothing = jnp.zeros_like(top)
    codes = jnp.stack([top, low, nothing, nothing], 2).reshape(n, 4 * slots)
    codes = jnp.broadcast_to(codes[:, :, None], (n, 4 * slots, LANES)).astype(BF16)
    live = alive.astype(F32)
    rays = beam.reshape(n, slots, 3, gate).astype(F32) * live[:, :, None, None]
    rays = jnp.pad(rays, ((0, 0), (0, 0), (0, 1), (0, 0)))
    own = jnp.arange(slots)[:, None] == jnp.arange(slots)[None, :]
    rays = jnp.where(own[None, :, None, :, None], rays[:, :, :, None, :], 0.0).reshape(n, 4 * slots, slots * gate)
    looked = (observed.reshape(n, slots, gate).astype(F32) * live[:, :, None]).reshape(n, 1, slots * gate)

    vmem = pl.BlockSpec(memory_space=pltpu.VMEM)
    hbm = pl.BlockSpec(memory_space=pl.ANY)
    message = pltpu.VMEM((n, 8, LANES), BF16)
    row = pltpu.VMEM((n, 1, LANES), F32)
    padded = pltpu.VMEM((3, nx + 2, nz, ny), F32)
    single = pltpu.VMEM((nx + 2, nz, ny), F32)
    wind, strain, cost = pl.pallas_call(
        functools.partial(kernel, sizes),
        name="wind_analysis",
        out_shape=(
            jax.ShapeDtypeStruct(background.shape, F32),
            jax.ShapeDtypeStruct((6, nx, nz, ny), F32),
            jax.ShapeDtypeStruct((1, LANES), F32),
        ),
        in_specs=[hbm, hbm, vmem, vmem, vmem],
        out_specs=(vmem, vmem, vmem),
        scratch_shapes=[
            pltpu.VMEM(interp.shape, BF16),
            padded, padded, padded, single, single,
            pltpu.VMEM((3, nx, nz, ny), F32),
            message, message, message, message, message, message, message, message, message, row, row,
            pltpu.VMEM((slots * n, blocks), BF16),
            pltpu.VMEM((blocks, slots * n), BF16),
            pltpu.VMEM((blocks, 3 * LANES), BF16),
            pltpu.VMEM((n, 1, slots * gate), F32),
            pltpu.VMEM((5, 2, nz, LANES), F32),
            pltpu.VMEM((5, 2, nz, LANES), F32),
            pltpu.SemaphoreType.DMA((6,)),
            pltpu.SemaphoreType.DMA((6,)),
            pltpu.SemaphoreType.DMA((5, 4)),
            pltpu.SemaphoreType.DMA((5, 4)),
            pltpu.SemaphoreType.DMA((2,)),
        ],
        compiler_params=pltpu.CompilerParams(
            collective_id=0, has_side_effects=True, vmem_limit_bytes=50 * 2**20),
    )(background, interp, codes, rays, looked)
    return wind, strain, cost[0, 1:3]


def solution(mesh):
    n_radar, n_tile = mesh.shape["radar"], mesh.shape["tile"]
    both = ("radar", "tile")
    in_specs = (
        P(None, "tile", None, "radar"), P(both, None, None), P(both, None, None),
        P(both, None), P(both), P(both, None))
    out_specs = (P(None, "tile", None, "radar"), P(None, "tile", None, "radar"), P())
    return jax.shard_map(
        functools.partial(shards, n_radar, n_tile), mesh=mesh, in_specs=in_specs, out_specs=out_specs, check_vma=False)
```

```python
import functools

import jax
import jax.numpy as jnp
from jax import lax
from jax.experimental import pallas as pl
from jax.experimental.pallas import tpu as pltpu
from jax.sharding import PartitionSpec as P

BACKGROUND_WEIGHT = 0.5
DIVERGENCE_WEIGHT = 1.0
STEP_LENGTH = 0.3
EPSILON = 1e-06
LANES = 128
F32 = jnp.float32
BF16 = jnp.bfloat16
LOGICAL = pl.DeviceIdType.LOGICAL
BACK, SPREAD0, GRAD0, SPREAD1, GRAD1 = range(5)


def iota(shape, dim):
    return lax.broadcasted_iota(jnp.int32, shape, dim)


def differences(nz, ny):
    sub = iota((nz, ny), 0)
    wide = iota((nz, ny), 1)

    def diff_z(v):
        up = jnp.where(sub == nz - 1, 0.0, pltpu.roll(v, nz - 1, 0))
        down = jnp.where(sub == 0, 0.0, pltpu.roll(v, 1, 0))
        return 0.5 * (up - down)

    def diff_y(v, low, high, x, k):
        at = 8 * x + k
        low = pltpu.roll(low, lax.rem(LANES - at, LANES), 1)
        high = pltpu.roll(high, LANES - 1 - at, 1)
        up = jnp.where(wide == ny - 1, jnp.concatenate([high] * (ny // LANES), 1), pltpu.roll(v, ny - 1, 1))
        down = jnp.where(wide == 0, jnp.concatenate([low] * (ny // LANES), 1), pltpu.roll(v, 1, 1))
        return 0.5 * (up - down)

    return diff_y, diff_z


def kernel(sizes, block_ref, count_ref, bg_hbm, interp_hbm, beam_hbm, looked_hbm,
           wind_ref, edges_ref, cost_ref,
           weights, beams16, looked16, wind, grad0, grad1, spread0, spread1, push,
           codes_out, codes_in, out1, in1, out2, in2, out3, in3, out4, in4, out5, in5,
           pick, place, field, beams32, looked32, rays, looked, misfit0, edges_out, edges_in,
           send_sems, recv_sems, halo_send, halo_recv, local_sems):
    n_radar, n_tile, total_cells, total_gates = sizes
    n = n_radar * n_tile
    nx, nz, ny = wind.shape[1] - 2, wind.shape[2], wind.shape[3]
    half = nx * nz
    group = min(16, n // 2)
    r, t = lax.axis_index("radar"), lax.axis_index("tile")
    me = r * n_tile + t
    other = jnp.where(me + 1 >= n, me + 1 - n, me + 1)

    load_bg = pltpu.make_async_copy(bg_hbm, wind.at[:, pl.ds(1, nx)], local_sems.at[0])
    load_interp = pltpu.make_async_copy(interp_hbm, weights, local_sems.at[1])
    load_beams = pltpu.make_async_copy(beam_hbm, beams16, local_sems.at[2])
    load_looked = pltpu.make_async_copy(looked_hbm, looked16, local_sems.at[3])
    load_bg.start()
    load_beams.start()
    load_looked.start()
    load_interp.start()

    barrier = pltpu.get_barrier_semaphore()

    def greet(k, carry):
        d = me + k
        d = jnp.where(d >= n, d - n, d)
        pl.semaphore_signal(barrier, inc=1, device_id=d, device_id_type=LOGICAL)
        return carry

    lax.fori_loop(1, n, greet, 0)

    def around(k):
        d = me + k
        return jnp.where(d >= n, d - n, d)

    def back_from(k):
        d = me - k
        return jnp.where(d < 0, d + n, d)

    lane = iota((nz, LANES), 1)

    def pack_edges(stage, source, comps, one_field):
        def plane(x, carry):
            low, high = carry
            for k in range(comps):
                if one_field:
                    a, b = source[x + 1, :, :LANES], source[x + 1, :, ny - LANES :]
                else:
                    a, b = source[k, x + 1, :, :LANES], source[k, x + 1, :, ny - LANES :]
                to = 8 * x + k
                a = pltpu.roll(a, to, 1)
                b = pltpu.roll(b, to + 1, 1)
                low = jnp.where(lane == to, a, low)
                high = jnp.where(lane == to, b, high)
            return low, high

        zero = jnp.zeros((nz, LANES), F32)
        low, high = lax.fori_loop(0, nx, plane, (zero, zero))
        edges_out[stage, 0] = low
        edges_out[stage, 1] = high

    def halo_copies(stage, array, one_field):
        def planes(x):
            return array.at[x] if one_field else array.at[:, x]

        def make(i, src, dst, device):
            return pltpu.make_async_remote_copy(
                src_ref=src, dst_ref=dst,
                send_sem=halo_send.at[stage, i], recv_sem=halo_recv.at[stage, i],
                device_id=device, device_id_type=LOGICAL)

        up_t = jnp.where(t < n_tile - 1, me + 1, me - 1)
        down_t = jnp.where(t > 0, me - 1, me + 1)
        up_r = jnp.where(r < n_radar - 1, me + n_tile, me - n_tile)
        down_r = jnp.where(r > 0, me - n_tile, me + n_tile)
        return (
            (t < n_tile - 1, t > 0, make(0, planes(nx), planes(0), up_t)),
            (t > 0, t < n_tile - 1, make(1, planes(1), planes(nx + 1), down_t)),
            (r < n_radar - 1, r > 0, make(2, edges_out.at[stage, 1], edges_in.at[stage, 0], up_r)),
            (r > 0, r < n_radar - 1, make(3, edges_out.at[stage, 0], edges_in.at[stage, 1], down_r)),
        )

    def send_halos(stage, array, one_field=False):
        for i, (sends, receives, copy) in enumerate(halo_copies(stage, array, one_field)):
            pl.when(sends)(copy.start)

            @pl.when(jnp.logical_not(receives))
            def _():
                if i >= 2:
                    edges_in[stage, i - 2] = jnp.zeros((nz, LANES), F32)
                elif one_field:
                    array[(nx + 1) * i] = jnp.zeros((nz, ny), F32)
                else:
                    array[:, (nx + 1) * i] = jnp.zeros((3, nz, ny), F32)

    def await_halos(stage, array, one_field=False):
        for sends, receives, copy in halo_copies(stage, array, one_field):
            pl.when(sends)(copy.wait_send)
            pl.when(receives)(copy.wait_recv)

    def exchange_copy(stage, src, dst, d, part):
        return pltpu.make_async_remote_copy(
            src_ref=src.at[d], dst_ref=dst.at[me],
            send_sem=send_sems.at[stage], recv_sem=recv_sems.at[stage, part],
            device_id=d, device_id_type=LOGICAL)

    def send_all(stage, src, dst, parts):
        def one(k, carry):
            exchange_copy(stage, src, dst, around(k), k // group if parts else 0).start()
            return carry

        lax.fori_loop(1, n, one, 0)
        dst[me] = src[me]

    def whole(stage, src, dst, part=0, count=n - 1):
        return pltpu.make_async_remote_copy(
            src_ref=src.at[pl.ds(0, count)], dst_ref=dst.at[pl.ds(0, count)],
            send_sem=send_sems.at[stage], recv_sem=recv_sems.at[stage, part],
            device_id=other, device_id_type=LOGICAL)

    diff_y, diff_z = differences(nz, ny)

    def divergence(stage, source, out):
        low, high = edges_in[stage, 0], edges_in[stage, 1]

        def plane(x, total):
            s = (0.5 * (source[0, x + 2] - source[0, x]) + diff_y(source[1, x + 1], low, high, x, 1)
                 + diff_z(source[2, x + 1]))
            out[x + 1] = s
            return total + s * s

        return lax.fori_loop(0, nx, plane, jnp.zeros((nz, ny), F32))

    def pushes(stage, source, x, low, high):
        v = source[x + 1]
        return (0.5 * (source[x] - source[x + 2]), -diff_y(v, low, high, x, 0), -diff_z(v))

    def total_of(v):
        return jnp.sum(jnp.sum(v, axis=0, keepdims=True), axis=1, keepdims=True)

    def to_field(source):
        for h in range(ny // LANES):
            for k in range(3):
                v = source[k, 1 : nx + 1, :, h * LANES : (h + 1) * LANES]
                field[h * half : (h + 1) * half, k * LANES : (k + 1) * LANES] = v.reshape(half, LANES).astype(BF16)

    def gather(out, extra):
        chosen = jnp.dot(pick[...], field[...], preferred_element_type=F32)
        zero = jnp.zeros((n, LANES), F32)
        rows = []
        for k in range(2):
            for c in range(3):
                rows.append(chosen[k * n : (k + 1) * n, c * LANES : (c + 1) * LANES])
            rows.append(zero if k == 1 or extra is None else jnp.broadcast_to(extra, (n, LANES)))
        out[...] = jnp.swapaxes(jnp.stack(rows, 0), 0, 1).astype(BF16)

    def observe(source, out, dst, stage, step):
        def some(q, cost, first):
            ds = [back_from(q * group + u) for u in range(group)]
            both = [weights[pl.ds(2 * d, 2)].reshape(2 * LANES, LANES) for d in ds]
            projected = [
                lax.dot_general(source[d], w, (((1,), (1,)), ((), ())), preferred_element_type=F32)
                for d, w in zip(ds, both)]
            beams = [rays[d] for d in ds]
            radial = [jnp.sum(b * p, axis=0, keepdims=True) for b, p in zip(beams, projected)]
            if step is None:
                misfit = [x - looked[d] for d, x in zip(ds, radial)]
                for d, x in zip(ds, misfit):
                    misfit0[d] = x
            else:
                misfit = [misfit0[d] - step * x for d, x in zip(ds, radial)]
            for x in misfit:
                cost = cost + x * x
            adjoint = [(b * x).astype(BF16) for b, x in zip(beams, misfit)]
            back = [jnp.dot(x, w, preferred_element_type=F32) for x, w in zip(adjoint, both)]
            for d, x in zip(ds, back):
                out[d] = x.astype(BF16)
            for u, d in enumerate(ds):
                if first and u == 0:
                    dst[d] = out[d]
                else:
                    exchange_copy(stage, out, dst, d, 0).start()
            return cost

        def later(q, cost):
            if step is None:
                whole(stage - 1, out, source, q, group).wait_recv()
            return some(q, cost, False)

        cost = jnp.zeros((1, 2 * LANES), F32)
        if step is None:
            whole(stage - 1, out, source, 0, group - 1).wait_recv()
        cost = some(0, cost, True)
        cost = lax.fori_loop(1, n // group, later, cost)
        return 0.5 * jnp.sum(cost, axis=1, keepdims=True)

    def scatter(source, out, to_field):
        rows = jnp.swapaxes(source[...].astype(F32), 0, 1).astype(BF16)
        landed = jnp.concatenate(
            [jnp.concatenate([rows[4 * k + c] for c in range(3)], 1) for k in range(2)], 0)
        total = jnp.zeros((nz, LANES), F32)
        for h in range(ny // LANES):
            added = jnp.dot(place[h * half : (h + 1) * half], landed, preferred_element_type=F32)
            for c in range(3):
                lanes = slice(h * LANES, (h + 1) * LANES)
                v = added[:, c * LANES : (c + 1) * LANES].reshape(nx, nz, LANES) + push[c, :, :, lanes]
                out[c, 1 : nx + 1, :, lanes] = v
                total = total + jnp.sum(v * v, axis=0)
                if to_field:
                    field[h * half : (h + 1) * half, c * LANES : (c + 1) * LANES] = v.reshape(half, LANES).astype(BF16)
        return total_of(total)

    def code_row(d, carry):
        count = count_ref[0, d]

        def code(k):
            b = block_ref[2 * d + k]
            c = lax.rem(b, ny // LANES) * half + lax.div(b, ny // LANES)
            return jnp.where(k < count, c, -1)

        codes_out[d] = jnp.where(iota((1, LANES), 1) < LANES // 2, code(0), code(1))
        return carry

    lax.fori_loop(0, n, code_row, 0)
    load_bg.wait()
    pack_edges(BACK, wind, 3, False)
    pl.semaphore_wait(barrier, n - 1)
    send_all(0, codes_out, codes_in, False)
    send_halos(BACK, wind)
    to_field(wind)

    load_beams.wait()
    load_looked.wait()
    beams32[...] = beams16[...].astype(F32)
    looked32[...] = looked16[...].astype(F32)
    zero = jnp.zeros((n, LANES), F32)
    rows = []
    for k in range(2):
        rows += [beams32[c, pl.ds(k, n, stride=2), :] for c in range(3)] + [zero]
    out_row = jnp.swapaxes(jnp.stack(rows, 0), 0, 1)
    rays[:, :, :LANES] = out_row
    eight = iota((8, LANES), 0)

    def ray_rows(q, carry):
        ds = [q * 8 + u for u in range(8)]
        counts = [count_ref[0, d] for d in ds]
        values = [rays[d, :, :LANES] for d in ds]
        seen = [[looked32[pl.ds(2 * d + k, 1), :] for k in range(2)] for d in ds]
        for d, count, v, s in zip(ds, counts, values, seen):
            rays[d, :, :LANES] = jnp.where((eight < 4) & (count > 0), v, 0.0)
            rays[d, :, LANES:] = jnp.where((eight >= 4) & (count > 1), v, 0.0)
            looked[d] = jnp.concatenate([jnp.where(count > k, s[k], 0.0) for k in range(2)], 1)
        return carry

    lax.fori_loop(0, n // 8, ray_rows, 0)

    whole(0, codes_out, codes_in).wait_recv()
    codes = codes_in[...].reshape(n, LANES)
    turned = pltpu.roll(codes, LANES // 2, 1)
    front = iota((n, LANES), 1) < LANES // 2
    code = (jnp.where(front, codes, turned), jnp.where(front, turned, codes))
    for k in range(2):
        for j in range(pick.shape[1] // LANES):
            hit = code[k] == iota((n, LANES), 1) + j * LANES
            pick[k * n : (k + 1) * n, j * LANES : (j + 1) * LANES] = jnp.where(hit, 1.0, 0.0).astype(BF16)

    gather(out1, None)
    send_all(1, out1, in1, True)
    for k in range(2):
        across = jnp.transpose(code[k])
        for j in range(pick.shape[1] // LANES):
            hit = across == iota((LANES, n), 0) + j * LANES
            place[j * LANES : (j + 1) * LANES, k * n : (k + 1) * n] = jnp.where(hit, 1.0, 0.0).astype(BF16)
    await_halos(BACK, wind)
    spread_cost0 = 0.5 * DIVERGENCE_WEIGHT * total_of(divergence(BACK, wind, spread0))
    pack_edges(SPREAD0, spread0, 1, True)
    send_halos(SPREAD0, spread0, True)
    load_interp.wait()
    cost0 = observe(in1, out2, in2, 2, None) + spread_cost0
    await_halos(SPREAD0, spread0, True)
    low, high = edges_in[SPREAD0, 0], edges_in[SPREAD0, 1]

    def push_plane(x, carry):
        for c, v in enumerate(pushes(SPREAD0, spread0, x, low, high)):
            push[c, x] = DIVERGENCE_WEIGHT * v
        return carry

    lax.fori_loop(0, nx, push_plane, 0)
    whole(2, out2, in2).wait_recv()
    squares = scatter(in2, grad0, True)

    first = squares.astype(BF16)
    rest = squares - first.astype(F32)
    second = rest.astype(BF16)
    third = (rest - second.astype(F32)).astype(BF16)
    at = iota((1, LANES), 1)
    extra = jnp.where(at == 0, first.astype(F32), jnp.where(at == 1, second.astype(F32), jnp.where(at == 2, third.astype(F32), 0.0)))
    gather(out3, extra)
    send_all(3, out3, in3, False)
    pack_edges(GRAD0, grad0, 3, False)
    send_halos(GRAD0, grad0)
    whole(3, out3, in3).wait_recv()
    squares = jnp.sum(jnp.sum(in3[...].astype(F32), axis=0)[3:4], axis=1, keepdims=True)
    step0 = STEP_LENGTH / jnp.sqrt(squares / total_cells + EPSILON)
    cost1 = observe(in3, out4, in4, 4, step0)
    await_halos(GRAD0, grad0)
    divergence(GRAD0, grad0, spread1)
    pack_edges(SPREAD1, spread1, 1, True)
    send_halos(SPREAD1, spread1, True)

    def wind_plane(x, carry):
        for c in range(3):
            wind[c, x] = wind[c, x] - step0 * grad0[c, x]
        return carry

    lax.fori_loop(0, nx + 2, wind_plane, 0)
    await_halos(SPREAD1, spread1, True)
    low1, high1 = edges_in[SPREAD1, 0], edges_in[SPREAD1, 1]

    def update_plane(x, carry):
        offsets, spreads = carry
        for c, v in enumerate(pushes(SPREAD1, spread1, x, low1, high1)):
            offset = -step0 * grad0[c, x + 1]
            offsets = offsets + offset * offset
            push[c, x] = push[c, x] - step0 * (DIVERGENCE_WEIGHT * v) + BACKGROUND_WEIGHT * offset
        spread = spread0[x + 1] - step0 * spread1[x + 1]
        return offsets, spreads + spread * spread

    zero = jnp.zeros((nz, ny), F32)
    offsets, spreads = lax.fori_loop(0, nx, update_plane, (zero, zero))
    cost1 = cost1 + 0.5 * total_of(BACKGROUND_WEIGHT * offsets + DIVERGENCE_WEIGHT * spreads)
    whole(4, out4, in4).wait_recv()
    squares = scatter(in4, grad1, False)

    summary = jnp.where(at == 0, squares, jnp.where(at == 1, cost0, jnp.where(at == 2, cost1, 0.0)))

    def fill(d, carry):
        out5[d] = summary
        return carry

    lax.fori_loop(0, n, fill, 0)
    send_all(5, out5, in5, False)
    pack_edges(GRAD1, grad1, 3, False)
    send_halos(GRAD1, grad1)
    whole(5, out5, in5).wait_recv()
    sums = jnp.sum(in5[...], axis=0)
    cost_ref[...] = sums / total_gates
    squares = jnp.sum(jnp.where(at == 0, sums, 0.0), axis=1, keepdims=True)
    step1 = STEP_LENGTH / jnp.sqrt(squares / total_cells + EPSILON)
    await_halos(GRAD1, grad1)

    def last_plane(x, carry):
        for c in range(3):
            wind_ref[c, x] = wind[c, x] - step1 * grad1[c, x]
        return carry

    lax.fori_loop(0, nx + 2, last_plane, 0)
    for i in range(2):
        edges_ref[i] = edges_in[BACK, i] - step0 * edges_in[GRAD0, i] - step1 * edges_in[GRAD1, i]

    pairs = ((codes_out, codes_in), (out1, in1), (out2, in2), (out3, in3), (out4, in4), (out5, in5))
    for stage, (src, dst) in enumerate(pairs):
        whole(stage, src, dst).wait_send()


def strain_kernel(planes, cost_ref, wind_ref, edges_ref, final_ref, strain_ref, trace_ref):
    nz, ny = wind_ref.shape[2:]
    start = pl.program_id(0) * planes
    diff_y, diff_z = differences(nz, ny)
    low, high = edges_ref[0], edges_ref[1]
    trace_ref[0] = cost_ref[0, 1]
    trace_ref[1] = cost_ref[0, 2]

    def plane(i, carry):
        x = start + i
        v = [wind_ref[c, x + 1] for c in range(3)]
        dx = [0.5 * (wind_ref[c, x + 2] - wind_ref[c, x]) for c in range(3)]
        dy = [diff_y(v[c], low, high, x, c) for c in range(3)]
        dz = [diff_z(v[c]) for c in range(3)]
        for c in range(3):
            final_ref[c, i] = v[c]
        strain_ref[0, i] = dx[0]
        strain_ref[1, i] = dy[1]
        strain_ref[2, i] = dz[2]
        strain_ref[3, i] = 0.5 * (dy[0] + dx[1])
        strain_ref[4, i] = 0.5 * (dz[0] + dx[2])
        strain_ref[5, i] = 0.5 * (dz[1] + dy[2])
        return carry

    lax.fori_loop(0, planes, plane, 0)


def shards(n_radar, n_tile, background, interp, beam, observed, cell_block, sweep_count):
    n = n_radar * n_tile
    _, nx, nz, ny = background.shape
    slots = interp.shape[0] // n
    gate = interp.shape[1]
    blocks = nx * nz * ny // gate
    total_cells = 3 * nx * nz * ny * n
    total_gates = interp.shape[0] * n * gate
    sizes = (n_radar, n_tile, total_cells, total_gates)

    vmem = pl.BlockSpec(memory_space=pltpu.VMEM)
    smem = pl.BlockSpec(memory_space=pltpu.SMEM)
    hbm = pl.BlockSpec(memory_space=pl.ANY)
    message = pltpu.VMEM((n, 8, LANES), BF16)
    row = pltpu.VMEM((n, 1, LANES), F32)
    code_row = pltpu.VMEM((n, 1, LANES), jnp.int32)
    padded = pltpu.VMEM((3, nx + 2, nz, ny), F32)
    single = pltpu.VMEM((nx + 2, nz, ny), F32)
    rays = jnp.transpose(beam, (1, 0, 2))
    groups = n // min(16, n // 2)
    wind, edges, cost = pl.pallas_call(
        functools.partial(kernel, sizes),
        name="wind_analysis",
        out_shape=(
            jax.ShapeDtypeStruct((3, nx + 2, nz, ny), F32),
            jax.ShapeDtypeStruct((2, nz, LANES), F32),
            jax.ShapeDtypeStruct((1, LANES), F32),
        ),
        in_specs=[smem, smem, hbm, hbm, hbm, hbm],
        out_specs=(vmem, vmem, vmem),
        scratch_shapes=[
            pltpu.VMEM(interp.shape, BF16),
            pltpu.VMEM(rays.shape, BF16),
            pltpu.VMEM(observed.shape, BF16),
            padded, padded, padded, single, single,
            pltpu.VMEM((3, nx, nz, ny), F32),
            code_row, code_row, message, message, message, message, message, message, message, message, row, row,
            pltpu.VMEM((slots * n, blocks), BF16),
            pltpu.VMEM((blocks, slots * n), BF16),
            pltpu.VMEM((blocks, 3 * LANES), BF16),
            pltpu.VMEM(rays.shape, F32),
            pltpu.VMEM(observed.shape, F32),
            pltpu.VMEM((n, 8, slots * gate), F32),
            pltpu.VMEM((n, 1, slots * gate), F32),
            pltpu.VMEM((n, 1, slots * gate), F32),
            pltpu.VMEM((5, 2, nz, LANES), F32),
            pltpu.VMEM((5, 2, nz, LANES), F32),
            pltpu.SemaphoreType.DMA((6,)),
            pltpu.SemaphoreType.DMA((6, groups)),
            pltpu.SemaphoreType.DMA((5, 4)),
            pltpu.SemaphoreType.DMA((5, 4)),
            pltpu.SemaphoreType.DMA((4,)),
        ],
        compiler_params=pltpu.CompilerParams(
            collective_id=0, has_side_effects=True, vmem_limit_bytes=50 * 2**20),
    )(cell_block, sweep_count, background, interp, rays, observed)

    planes = nx // 4
    return pl.pallas_call(
        functools.partial(strain_kernel, planes),
        name="strain",
        grid=(nx // planes,),
        out_shape=(
            jax.ShapeDtypeStruct(background.shape, F32),
            jax.ShapeDtypeStruct((6, nx, nz, ny), F32),
            jax.ShapeDtypeStruct((2,), F32),
        ),
        in_specs=[smem, vmem, vmem],
        out_specs=(
            pl.BlockSpec((3, planes, nz, ny), lambda i: (0, i, 0, 0)),
            pl.BlockSpec((6, planes, nz, ny), lambda i: (0, i, 0, 0)),
            smem,
        ),
        compiler_params=pltpu.CompilerParams(vmem_limit_bytes=24 * 2**20),
    )(cost, wind, edges)


def solution(mesh):
    n_radar, n_tile = mesh.shape["radar"], mesh.shape["tile"]
    both = ("radar", "tile")
    in_specs = (
        P(None, "tile", None, "radar"), P(both, None, None), P(both, None, None),
        P(both, None), P(both), P(both, None))
    out_specs = (P(None, "tile", None, "radar"), P(None, "tile", None, "radar"), P())
    return jax.shard_map(
        functools.partial(shards, n_radar, n_tile), mesh=mesh, in_specs=in_specs, out_specs=out_specs, check_vma=False)
```

```python
import functools

import jax
import jax.numpy as jnp
from jax import lax
from jax.experimental import pallas as pl
from jax.experimental.pallas import tpu as pltpu
from jax.sharding import PartitionSpec as P

BACKGROUND_WEIGHT = 0.5
DIVERGENCE_WEIGHT = 1.0
STEP_LENGTH = 0.3
EPSILON = 1e-06
LANES = 128
F32 = jnp.float32
BF16 = jnp.bfloat16
LOGICAL = pl.DeviceIdType.LOGICAL
BACK, SPREAD0, GRAD0, SPREAD1, GRAD1, REST0 = range(6)


def iota(shape, dim):
    return lax.broadcasted_iota(jnp.int32, shape, dim)


def differences(nz, ny):
    sub = iota((nz, ny), 0)
    wide = iota((nz, ny), 1)

    def diff_z(v):
        up = jnp.where(sub == nz - 1, 0.0, pltpu.roll(v, nz - 1, 0))
        down = jnp.where(sub == 0, 0.0, pltpu.roll(v, 1, 0))
        return 0.5 * (up - down)

    def diff_y(v, low, high, x, k):
        at = 8 * x + k
        low = pltpu.roll(low, (LANES - at) % LANES if isinstance(at, int) else lax.rem(LANES - at, LANES), 1)
        high = pltpu.roll(high, LANES - 1 - at, 1)
        up = jnp.where(wide == ny - 1, jnp.concatenate([high] * (ny // LANES), 1), pltpu.roll(v, ny - 1, 1))
        down = jnp.where(wide == 0, jnp.concatenate([low] * (ny // LANES), 1), pltpu.roll(v, 1, 1))
        return 0.5 * (up - down)

    return diff_y, diff_z


def kernel(sizes, torus, block_hbm, count_hbm, bg_hbm, interp_hbm, beam_hbm, looked_hbm,
           wind_out, grad_out, info_out,
           weights, beams16, looked16, wind, grad0, grad1, spread0, spread1, push,
           block_ref, count_ref, codes_out, codes_in, out1, in1, out2, in2, out3, in3, out4, in4, out5, in5,
           info, pick, place, field, beams32, looked32, rays, looked, misfit0, held, edges_out, edges_in,
           send_sems, recv_sems, halo_send, halo_recv, local_sems):
    n_radar, n_tile, total_cells, total_gates = sizes
    n = n_radar * n_tile
    nx, nz, ny = wind.shape[1] - 2, wind.shape[2], wind.shape[3]
    half = nx * nz
    group = min(16, n // 2)
    r, t = lax.axis_index("radar"), lax.axis_index("tile")
    me = r * n_tile + t
    other = jnp.where(me + 1 >= n, me + 1 - n, me + 1)

    load_bg = pltpu.make_async_copy(bg_hbm, wind.at[:, pl.ds(1, nx)], local_sems.at[0])
    load_interp = pltpu.make_async_copy(interp_hbm, weights, local_sems.at[1])
    load_blocks = pltpu.make_async_copy(block_hbm, block_ref, local_sems.at[4])
    load_counts = pltpu.make_async_copy(count_hbm, count_ref, local_sems.at[5])
    load_beams = pltpu.make_async_copy(beam_hbm, beams16, local_sems.at[2])
    load_looked = pltpu.make_async_copy(looked_hbm, looked16, local_sems.at[3])
    load_blocks.start()
    load_counts.start()
    load_bg.start()
    load_beams.start()
    load_looked.start()
    load_interp.start()

    cores, ys, zs = torus
    xs = n_radar // cores
    rounds, turns = xs * ys, zs * cores

    def distance(i, size):
        if size == 1:
            return 0
        return jnp.where(i == size - 1, 0, jnp.where(i == 0, size // 2, i + lax.div(i, 2)))

    def round_base(i, sign):
        a, b = distance(lax.div(i, ys), xs), distance(lax.rem(i, ys), ys)
        x = lax.rem(lax.div(r, cores) + xs + sign * a, xs)
        y = lax.rem(lax.div(t, zs) + ys + sign * b, ys)
        return x * (cores * n_tile) + y * zs

    hops = sorted([(c, e) for c in range(zs) for e in range(cores)], key=lambda s: -min(s[0], zs - s[0]) - 0.5 * s[1])
    turn_base = {
        sign: [lax.rem(t + zs + sign * c, zs) + lax.rem(r + cores + sign * e, cores) * n_tile for c, e in hops]
        for sign in (1, -1)}

    def for_others(action):
        def one_round(i, carry):
            base = round_base(i, 1)
            for j in range(turns):
                action(i * turns + j, base + turn_base[1][j])
            return carry

        lax.fori_loop(0, rounds - 1, one_round, 0)
        base = round_base(rounds - 1, 1)
        for j in range(turns - 1):
            action((rounds - 1) * turns + j, base + turn_base[1][j])

    barrier = pltpu.get_barrier_semaphore()

    for_others(lambda k, d: pl.semaphore_signal(barrier, inc=1, device_id=d, device_id_type=LOGICAL))

    def over_planes(count, body, carry, at_once=2):
        def some(i, carry):
            stores = []
            for u in range(at_once):
                new, carry = body(i * at_once + u, carry)
                stores += new
            for ref, index, value in stores:
                ref[index] = value
            return carry

        return lax.fori_loop(0, count // at_once, some, carry)

    lane = iota((nz, LANES), 1)

    def pack_edges(stage, source, comps, one_field):
        def plane(x, carry):
            low, high = carry
            for k in range(comps):
                if one_field:
                    a, b = source[x + 1, :, :LANES], source[x + 1, :, ny - LANES :]
                else:
                    a, b = source[k, x + 1, :, :LANES], source[k, x + 1, :, ny - LANES :]
                to = 8 * x + k
                a = pltpu.roll(a, to, 1)
                b = pltpu.roll(b, to + 1, 1)
                low = jnp.where(lane == to, a, low)
                high = jnp.where(lane == to, b, high)
            return [], (low, high)

        zero = jnp.zeros((nz, LANES), F32)
        low, high = over_planes(nx, plane, (zero, zero), 4)
        edges_out[stage, 0] = low
        edges_out[stage, 1] = high

    def chosen_planes(array, x, part):
        if part == "one":
            return array.at[x]
        return array.at[{"all": pl.ds(0, 3), "first": pl.ds(0, 1), "rest": pl.ds(1, 2)}[part], x]

    def halo_copies(stage, array, part):
        def make(i, src, dst, device):
            return pltpu.make_async_remote_copy(
                src_ref=src, dst_ref=dst,
                send_sem=halo_send.at[stage, i], recv_sem=halo_recv.at[stage, i],
                device_id=device, device_id_type=LOGICAL)

        up_t = jnp.where(t < n_tile - 1, me + 1, me - 1)
        down_t = jnp.where(t > 0, me - 1, me + 1)
        up_r = jnp.where(r < n_radar - 1, me + n_tile, me - n_tile)
        down_r = jnp.where(r > 0, me - n_tile, me + n_tile)
        planes = functools.partial(chosen_planes, array, part=part)
        copies = [
            (t < n_tile - 1, t > 0, make(0, planes(nx), planes(0), up_t)),
            (t > 0, t < n_tile - 1, make(1, planes(1), planes(nx + 1), down_t)),
        ]
        if part != "rest":
            copies += [
                (r < n_radar - 1, r > 0, make(2, edges_out.at[stage, 1], edges_in.at[stage, 0], up_r)),
                (r > 0, r < n_radar - 1, make(3, edges_out.at[stage, 0], edges_in.at[stage, 1], down_r)),
            ]
        return copies

    def send_halos(stage, array, part="all"):
        for i, (sends, receives, copy) in enumerate(halo_copies(stage, array, part)):
            pl.when(sends)(copy.start)

            @pl.when(jnp.logical_not(receives))
            def _():
                if i >= 2:
                    edges_in[stage, i - 2] = jnp.zeros((nz, LANES), F32)
                else:
                    plane = chosen_planes(array, (nx + 1) * i, part)
                    plane[...] = jnp.zeros(plane.shape, F32)

    def await_halos(stage, array, part="all"):
        for sends, receives, copy in halo_copies(stage, array, part):
            pl.when(sends)(copy.wait_send)
            pl.when(receives)(copy.wait_recv)

    def exchange_copy(stage, src, dst, d, part):
        return pltpu.make_async_remote_copy(
            src_ref=src.at[d], dst_ref=dst.at[me],
            send_sem=send_sems.at[stage], recv_sem=recv_sems.at[stage, part],
            device_id=d, device_id_type=LOGICAL)

    def send_all(stage, src, dst, parts):
        for_others(lambda k, d: exchange_copy(stage, src, dst, d, k // group if parts else 0).start())
        dst[me] = src[me]

    def whole(stage, src, dst, part=0, count=n - 1):
        return pltpu.make_async_remote_copy(
            src_ref=src.at[pl.ds(0, count)], dst_ref=dst.at[pl.ds(0, count)],
            send_sem=send_sems.at[stage], recv_sem=recv_sems.at[stage, part],
            device_id=other, device_id_type=LOGICAL)

    diff_y, diff_z = differences(nz, ny)

    def divergence(stage, source, out):
        low, high = edges_in[stage, 0], edges_in[stage, 1]

        def plane(x, total):
            s = (0.5 * (source[0, x + 2] - source[0, x]) + diff_y(source[1, x + 1], low, high, x, 1)
                 + diff_z(source[2, x + 1]))
            return [(out, x + 1, s)], total + s * s

        return over_planes(nx, plane, jnp.zeros((nz, ny), F32))

    def pushes(stage, source, x, low, high):
        v = source[x + 1]
        return (0.5 * (source[x] - source[x + 2]), -diff_y(v, low, high, x, 0), -diff_z(v))

    def total_of(v):
        return jnp.sum(jnp.sum(v, axis=0, keepdims=True), axis=1, keepdims=True)

    def to_field(source):
        for h in range(ny // LANES):
            for k in range(3):
                v = source[k, 1 : nx + 1, :, h * LANES : (h + 1) * LANES]
                field[h * half : (h + 1) * half, k * LANES : (k + 1) * LANES] = v.reshape(half, LANES).astype(BF16)

    def gather(out, extra):
        chosen = jnp.dot(pick[...], field[...], preferred_element_type=F32)
        zero = jnp.zeros((n, LANES), F32)
        rows = []
        for k in range(2):
            for c in range(3):
                rows.append(chosen[k * n : (k + 1) * n, c * LANES : (c + 1) * LANES])
            rows.append(zero if k == 1 or extra is None else jnp.broadcast_to(extra, (n, LANES)))
        out[...] = jnp.swapaxes(jnp.stack(rows, 0), 0, 1).astype(BF16)

    def observe(source, out, dst, stage, step):
        count = n // group

        def members(q):
            bases = [round_base(q * (group // turns) + i, -1) for i in range(group // turns)]
            return [base + j for base in bases for j in turn_base[-1]]

        def weights_of(d):
            return weights[pl.ds(2 * d, 2)].reshape(2 * LANES, LANES)

        def project(ds):
            return [
                lax.dot_general(source[d], weights_of(d), (((1,), (1,)), ((), ())), preferred_element_type=F32)
                for d in ds]

        def adjoints(ds, projected, cost):
            beams = [rays[d] for d in ds]
            radial = [jnp.sum(b * p, axis=0, keepdims=True) for b, p in zip(beams, projected)]
            if step is None:
                misfit = [x - looked[d] for d, x in zip(ds, radial)]
                for d, x in zip(ds, misfit):
                    misfit0[d] = x
            else:
                misfit = [misfit0[d] - step * x for d, x in zip(ds, radial)]
            for x in misfit:
                cost = cost + x * x
            for u, (b, x) in enumerate(zip(beams, misfit)):
                held[u] = (b * x).astype(BF16)
            return cost

        def back(ds):
            return [jnp.dot(held[u], weights_of(d), preferred_element_type=F32) for u, d in enumerate(ds)]

        def send(ds, values, last):
            for d, x in zip(ds, values):
                out[d] = x.astype(BF16)
            for u, d in enumerate(ds):
                if last and u == group - 1:
                    dst[me] = out[me]
                else:
                    exchange_copy(stage, out, dst, d, 0).start()

        def arrive(q, last):
            if step is None:
                whole(stage - 1, out, source, q, group - last).wait_recv()

        def middle(q, cost, last=False):
            ds, ahead = members(q), members(q + 1)
            arrive(q + 1, last)
            values = back(ds)
            projected = project(ahead)
            send(ds, values, False)
            return adjoints(ahead, projected, cost)

        arrive(0, 0)
        first = members(0)
        cost = adjoints(first, project(first), jnp.zeros((1, 2 * LANES), F32))
        cost = lax.fori_loop(0, count - 2, middle, cost)
        cost = middle(count - 2, cost, True)
        final = members(count - 1)
        send(final, back(final), True)
        return 0.5 * jnp.sum(cost, axis=1, keepdims=True)

    def scatter(source, out, to_field):
        rows = jnp.swapaxes(source[...].astype(F32), 0, 1).astype(BF16)
        landed = jnp.concatenate(
            [jnp.concatenate([rows[4 * k + c] for c in range(3)], 1) for k in range(2)], 0)
        total = jnp.zeros((nz, LANES), F32)
        for h in range(ny // LANES):
            added = jnp.dot(place[h * half : (h + 1) * half], landed, preferred_element_type=F32)
            for c in range(3):
                lanes = slice(h * LANES, (h + 1) * LANES)
                v = added[:, c * LANES : (c + 1) * LANES].reshape(nx, nz, LANES) + push[c, :, :, lanes]
                out[c, 1 : nx + 1, :, lanes] = v
                total = total + jnp.sum(v * v, axis=0)
                if to_field:
                    field[h * half : (h + 1) * half, c * LANES : (c + 1) * LANES] = v.reshape(half, LANES).astype(BF16)
        return total_of(total)

    ahead = iota((1, LANES), 1) < LANES // 2

    def code_rows(q, carry):
        ds = [q * 8 + u for u in range(8)]
        counts = [count_ref[0, d] for d in ds]
        blocks = [[block_ref[0, 2 * d + k] for k in range(2)] for d in ds]
        rows = []
        for count, pair in zip(counts, blocks):
            codes = [lax.rem(b, ny // LANES) * half + lax.div(b, ny // LANES) for b in pair]
            codes = [jnp.where(k < count, c, -1) for k, c in enumerate(codes)]
            rows.append(jnp.where(ahead, codes[0], codes[1]))
        for d, row in zip(ds, rows):
            codes_out[d] = row
        return carry

    load_blocks.wait()
    load_counts.wait()
    lax.fori_loop(0, n // 8, code_rows, 0)
    load_bg.wait()
    pack_edges(BACK, wind, 3, False)
    pl.semaphore_wait(barrier, n - 1)
    send_all(0, codes_out, codes_in, False)
    send_halos(BACK, wind)
    to_field(wind)

    load_beams.wait()
    load_looked.wait()
    beams32[...] = beams16[...].astype(F32)
    looked32[...] = looked16[...].astype(F32)
    zero = jnp.zeros((n, LANES), F32)
    rows = []
    for k in range(2):
        rows += [beams32[c, pl.ds(k, n, stride=2), :] for c in range(3)] + [zero]
    out_row = jnp.swapaxes(jnp.stack(rows, 0), 0, 1)
    rays[:, :, :LANES] = out_row
    eight = iota((8, LANES), 0)

    def ray_rows(q, carry):
        ds = [q * 8 + u for u in range(8)]
        counts = [count_ref[0, d] for d in ds]
        values = [rays[d, :, :LANES] for d in ds]
        seen = [[looked32[pl.ds(2 * d + k, 1), :] for k in range(2)] for d in ds]
        for d, count, v, s in zip(ds, counts, values, seen):
            rays[d, :, :LANES] = jnp.where((eight < 4) & (count > 0), v, 0.0)
            rays[d, :, LANES:] = jnp.where((eight >= 4) & (count > 1), v, 0.0)
            looked[d] = jnp.concatenate([jnp.where(count > k, s[k], 0.0) for k in range(2)], 1)
        return carry

    lax.fori_loop(0, n // 8, ray_rows, 0)

    whole(0, codes_out, codes_in).wait_recv()
    codes = codes_in[...].reshape(n, LANES)
    turned = pltpu.roll(codes, LANES // 2, 1)
    front = iota((n, LANES), 1) < LANES // 2
    code = (jnp.where(front, codes, turned), jnp.where(front, turned, codes))
    for k in range(2):
        for j in range(pick.shape[1] // LANES):
            hit = code[k] == iota((n, LANES), 1) + j * LANES
            pick[k * n : (k + 1) * n, j * LANES : (j + 1) * LANES] = jnp.where(hit, 1.0, 0.0).astype(BF16)

    gather(out1, None)
    send_all(1, out1, in1, True)
    for k in range(2):
        across = jnp.transpose(code[k])
        for j in range(pick.shape[1] // LANES):
            hit = across == iota((LANES, n), 0) + j * LANES
            place[j * LANES : (j + 1) * LANES, k * n : (k + 1) * n] = jnp.where(hit, 1.0, 0.0).astype(BF16)
    await_halos(BACK, wind)
    spread_cost0 = 0.5 * DIVERGENCE_WEIGHT * total_of(divergence(BACK, wind, spread0))
    pack_edges(SPREAD0, spread0, 1, True)
    send_halos(SPREAD0, spread0, "one")
    load_interp.wait()
    cost0 = observe(in1, out2, in2, 2, None) + spread_cost0
    await_halos(SPREAD0, spread0, "one")
    low, high = edges_in[SPREAD0, 0], edges_in[SPREAD0, 1]

    def push_plane(x, carry):
        values = pushes(SPREAD0, spread0, x, low, high)
        return [(push, (c, x), DIVERGENCE_WEIGHT * v) for c, v in enumerate(values)], carry

    over_planes(nx, push_plane, 0)
    whole(2, out2, in2).wait_recv()
    squares = scatter(in2, grad0, True)

    first = squares.astype(BF16)
    rest = squares - first.astype(F32)
    second = rest.astype(BF16)
    third = (rest - second.astype(F32)).astype(BF16)
    at = iota((1, LANES), 1)
    extra = jnp.where(at == 0, first.astype(F32), jnp.where(at == 1, second.astype(F32), jnp.where(at == 2, third.astype(F32), 0.0)))
    gather(out3, extra)
    pack_edges(GRAD0, grad0, 3, False)
    send_halos(GRAD0, grad0, "first")
    send_all(3, out3, in3, False)
    await_halos(GRAD0, grad0, "first")
    divergence(GRAD0, grad0, spread1)
    pack_edges(SPREAD1, spread1, 1, True)
    send_halos(SPREAD1, spread1, "one")
    whole(3, out3, in3).wait_recv()
    squares = jnp.sum(jnp.sum(in3[...].astype(F32), axis=0)[3:4], axis=1, keepdims=True)
    step0 = STEP_LENGTH / jnp.sqrt(squares / total_cells + EPSILON)
    cost1 = observe(in3, out4, in4, 4, step0)

    def wind_plane(x, carry):
        return [(wind, (c, x), wind[c, x] - step0 * grad0[c, x]) for c in range(3)], carry

    send_halos(REST0, grad0, "rest")
    await_halos(SPREAD1, spread1, "one")
    low1, high1 = edges_in[SPREAD1, 0], edges_in[SPREAD1, 1]

    def update_plane(x, carry):
        offsets, spreads = carry
        stores = []
        for c, v in enumerate(pushes(SPREAD1, spread1, x, low1, high1)):
            offset = -step0 * grad0[c, x + 1]
            offsets = offsets + offset * offset
            stores.append((push, (c, x), push[c, x] - step0 * (DIVERGENCE_WEIGHT * v) + BACKGROUND_WEIGHT * offset))
        spread = spread0[x + 1] - step0 * spread1[x + 1]
        return stores, (offsets, spreads + spread * spread)

    zero = jnp.zeros((nz, ny), F32)
    offsets, spreads = over_planes(nx, update_plane, (zero, zero))
    cost1 = cost1 + 0.5 * total_of(BACKGROUND_WEIGHT * offsets + DIVERGENCE_WEIGHT * spreads)
    await_halos(REST0, grad0, "rest")
    over_planes(nx + 2, wind_plane, 0)
    save_wind = pltpu.make_async_copy(wind, wind_out, local_sems.at[6])
    save_wind.start()
    whole(4, out4, in4).wait_recv()
    squares = scatter(in4, grad1, False)

    inner = pl.ds(1, nx)
    save_grad = pltpu.make_async_copy(grad1.at[:, inner], grad_out.at[:, inner], local_sems.at[7])
    summary = jnp.where(at == 0, squares, jnp.where(at == 1, cost0, jnp.where(at == 2, cost1, 0.0)))

    out5[...] = summary

    for_others(lambda k, d: pltpu.make_async_remote_copy(
        src_ref=out5, dst_ref=in5.at[me], send_sem=send_sems.at[5], recv_sem=recv_sems.at[5, 0],
        device_id=d, device_id_type=LOGICAL).start())
    in5[me] = summary
    save_grad.start()
    pack_edges(GRAD1, grad1, 3, False)
    send_halos(GRAD1, grad1)
    for i in range(2):
        info[i] = edges_in[BACK, i] - step0 * edges_in[GRAD0, i]
    info[4] = jnp.zeros((nz, LANES), F32)
    await_halos(GRAD1, grad1)
    for i in range(2):
        info[2 + i] = edges_in[GRAD1, i]
    save_edges = [
        pltpu.make_async_copy(grad1.at[:, x], grad_out.at[:, x], local_sems.at[9 + i])
        for i, x in enumerate((0, nx + 1))]
    for copy in save_edges:
        copy.start()
    whole(5, in5, in5).wait_recv()
    sums = jnp.sum(in5[...], axis=0)
    squares = jnp.sum(jnp.where(at == 0, sums, 0.0), axis=1, keepdims=True)
    step1 = STEP_LENGTH / jnp.sqrt(squares / total_cells + EPSILON)
    info[4, 0:1, :] = jnp.where(at == 0, step1, sums / total_gates)
    save_info = pltpu.make_async_copy(info, info_out, local_sems.at[8])
    save_info.start()
    save_info.wait()
    for copy in save_edges:
        copy.wait()
    save_grad.wait()
    save_wind.wait()

    pairs = ((codes_out, codes_in), (out1, in1), (out2, in2), (out3, in3), (out4, in4), (in5, in5))
    for stage, (src, dst) in enumerate(pairs):
        whole(stage, src, dst).wait_send()


def strain_kernel(wind_hbm, grad_hbm, info_hbm, final_hbm, strain_hbm, trace_ref,
                  wind, grad, info, strain, wind_sems, grad_sems, info_sem, final_sems, strain_sems):
    nx, nz, ny = wind.shape[1] - 2, wind.shape[2], wind.shape[3]
    diff_y, diff_z = differences(nz, ny)
    load_info = pltpu.make_async_copy(info_hbm, info, info_sem)
    load_info.start()
    starts = list(range(0, nx + 2, 4))
    loads = []
    for i, start in enumerate(starts):
        span = pl.ds(start, min(4, nx + 2 - start))
        loads.append((
            pltpu.make_async_copy(wind_hbm.at[:, span], wind.at[:, span], wind_sems.at[i]),
            pltpu.make_async_copy(grad_hbm.at[:, span], grad.at[:, span], grad_sems.at[i])))
        for copy in loads[-1]:
            copy.start()
    load_info.wait()
    step = info[4, 0:1, 0:1]
    low, high = (info[i] - step * info[2 + i] for i in range(2))
    scalars = info[4, 0:1, :]
    at = iota((1, LANES), 1)
    for i in range(2):
        trace_ref[i] = jnp.sum(jnp.where(at == i + 1, scalars, 0.0))

    ready, saves = 0, []
    for j in range(nx // 2):
        while ready < len(starts) and starts[ready] <= 2 * j + 3:
            for copy in loads[ready]:
                copy.wait()
            for x in range(starts[ready], min(starts[ready] + 4, nx + 2)):
                new = [wind[c, x] - step * grad[c, x] for c in range(3)]
                for c in range(3):
                    wind[c, x] = new[c]
            ready += 1
        stores = []
        for x in (2 * j, 2 * j + 1):
            v = [wind[c, x + 1] for c in range(3)]
            dx = [0.5 * (wind[c, x + 2] - wind[c, x]) for c in range(3)]
            dy = [diff_y(v[c], low, high, x, c) for c in range(3)]
            dz = [diff_z(v[c]) for c in range(3)]
            values = (dx[0], dy[1], dz[2], 0.5 * (dy[0] + dx[1]), 0.5 * (dz[0] + dx[2]), 0.5 * (dz[1] + dy[2]))
            stores += [(c, x, value) for c, value in enumerate(values)]
        for c, x, value in stores:
            strain[c, x] = value
        pair = pl.ds(2 * j, 2)
        saves += [
            pltpu.make_async_copy(wind.at[:, pl.ds(2 * j + 1, 2)], final_hbm.at[:, pair], final_sems.at[j]),
            pltpu.make_async_copy(strain.at[:, pair], strain_hbm.at[:, pair], strain_sems.at[j])]
        for copy in saves[-2:]:
            copy.start()
    for copy in saves:
        copy.wait()


def shards(n_radar, n_tile, background, interp, beam, observed, cell_block, sweep_count):
    n = n_radar * n_tile
    _, nx, nz, ny = background.shape
    slots = interp.shape[0] // n
    gate = interp.shape[1]
    blocks = nx * nz * ny // gate
    total_cells = 3 * nx * nz * ny * n
    total_gates = interp.shape[0] * n * gate
    sizes = (n_radar, n_tile, total_cells, total_gates)
    torus = (2, n_tile // 4, 4)

    smem = pl.BlockSpec(memory_space=pltpu.SMEM)
    hbm = pl.BlockSpec(memory_space=pltpu.HBM)
    message = pltpu.VMEM((n, 8, LANES), BF16)
    row = pltpu.VMEM((n, 1, LANES), F32)
    code_row = pltpu.VMEM((n, 1, LANES), jnp.int32)
    padded = pltpu.VMEM((3, nx + 2, nz, ny), F32)
    single = pltpu.VMEM((nx + 2, nz, ny), F32)
    rays = jnp.transpose(beam, (1, 0, 2))
    groups = n // min(16, n // 2)
    wind, grad, info = pl.pallas_call(
        functools.partial(kernel, sizes, torus),
        name="wind_analysis",
        out_shape=(
            jax.ShapeDtypeStruct((3, nx + 2, nz, ny), F32),
            jax.ShapeDtypeStruct((3, nx + 2, nz, ny), F32),
            jax.ShapeDtypeStruct((5, nz, LANES), F32),
        ),
        in_specs=[hbm] * 6,
        out_specs=(hbm, hbm, hbm),
        scratch_shapes=[
            pltpu.VMEM(interp.shape, BF16),
            pltpu.VMEM(rays.shape, BF16),
            pltpu.VMEM(observed.shape, BF16),
            padded, padded, padded, single, single,
            pltpu.VMEM((3, nx, nz, ny), F32),
            pltpu.SMEM((1, n * slots), jnp.int32), pltpu.SMEM((1, n), jnp.int32),
            code_row, code_row, message, message, message, message, message, message, message, message, pltpu.VMEM((1, LANES), F32), row,
            pltpu.VMEM((5, nz, LANES), F32),
            pltpu.VMEM((slots * n, blocks), BF16),
            pltpu.VMEM((blocks, slots * n), BF16),
            pltpu.VMEM((blocks, 3 * LANES), BF16),
            pltpu.VMEM(rays.shape, F32),
            pltpu.VMEM(observed.shape, F32),
            pltpu.VMEM((n, 8, slots * gate), F32),
            pltpu.VMEM((n, 1, slots * gate), F32),
            pltpu.VMEM((n, 1, slots * gate), F32),
            pltpu.VMEM((n // groups, 8, slots * gate), BF16),
            pltpu.VMEM((5, 2, nz, LANES), F32),
            pltpu.VMEM((5, 2, nz, LANES), F32),
            pltpu.SemaphoreType.DMA((6,)),
            pltpu.SemaphoreType.DMA((6, groups)),
            pltpu.SemaphoreType.DMA((6, 4)),
            pltpu.SemaphoreType.DMA((6, 4)),
            pltpu.SemaphoreType.DMA((11,)),
        ],
        compiler_params=pltpu.CompilerParams(
            collective_id=0, has_side_effects=True, vmem_limit_bytes=60 * 2**20),
    )(cell_block.reshape(1, n * slots), sweep_count, background, interp, rays, observed)

    spans = len(range(0, nx + 2, 4))
    return pl.pallas_call(
        strain_kernel,
        name="strain",
        out_shape=(
            jax.ShapeDtypeStruct(background.shape, F32),
            jax.ShapeDtypeStruct((6, nx, nz, ny), F32),
            jax.ShapeDtypeStruct((2,), F32),
        ),
        in_specs=[hbm] * 3,
        out_specs=(hbm, hbm, smem),
        scratch_shapes=[
            padded, padded, pltpu.VMEM((5, nz, LANES), F32), pltpu.VMEM((6, nx, nz, ny), F32),
            pltpu.SemaphoreType.DMA((spans,)), pltpu.SemaphoreType.DMA((spans,)), pltpu.SemaphoreType.DMA,
            pltpu.SemaphoreType.DMA((nx // 2,)), pltpu.SemaphoreType.DMA((nx // 2,))],
        compiler_params=pltpu.CompilerParams(vmem_limit_bytes=60 * 2**20),
    )(wind, grad, info)


def solution(mesh):
    n_radar, n_tile = mesh.shape["radar"], mesh.shape["tile"]
    both = ("radar", "tile")
    in_specs = (
        P(None, "tile", None, "radar"), P(both, None, None), P(both, None, None),
        P(both, None), P(both), P(both, None))
    out_specs = (P(None, "tile", None, "radar"), P(None, "tile", None, "radar"), P())
    return jax.shard_map(
        functools.partial(shards, n_radar, n_tile), mesh=mesh, in_specs=in_specs, out_specs=out_specs, check_vma=False)
```

```python
import functools

import jax
import jax.numpy as jnp
from jax import lax
from jax.experimental import pallas as pl
from jax.experimental.pallas import tpu as pltpu
from jax.sharding import PartitionSpec as P

BACKGROUND_WEIGHT = 0.5
DIVERGENCE_WEIGHT = 1.0
STEP_LENGTH = 0.3
EPSILON = 1e-06
LANES = 128
F32 = jnp.float32
BF16 = jnp.bfloat16
LOGICAL = pl.DeviceIdType.LOGICAL
BACK, SPREAD0, GRAD0, SPREAD1, GRAD1, REST0 = range(6)


def iota(shape, dim):
    return lax.broadcasted_iota(jnp.int32, shape, dim)


def differences(nz, ny):
    sub = iota((nz, ny), 0)
    wide = iota((nz, ny), 1)

    def diff_z(v):
        up = jnp.where(sub == nz - 1, 0.0, pltpu.roll(v, nz - 1, 0))
        down = jnp.where(sub == 0, 0.0, pltpu.roll(v, 1, 0))
        return 0.5 * (up - down)

    def diff_y(v, low, high, x, k):
        at = 8 * x + k
        low = pltpu.roll(low, (LANES - at) % LANES if isinstance(at, int) else lax.rem(LANES - at, LANES), 1)
        high = pltpu.roll(high, LANES - 1 - at, 1)
        up = jnp.where(wide == ny - 1, jnp.concatenate([high] * (ny // LANES), 1), pltpu.roll(v, ny - 1, 1))
        down = jnp.where(wide == 0, jnp.concatenate([low] * (ny // LANES), 1), pltpu.roll(v, 1, 1))
        return 0.5 * (up - down)

    return diff_y, diff_z


def kernel(sizes, torus, block_hbm, count_hbm, bg_hbm, interp_hbm, beam_hbm, looked_hbm,
           wind_out, grad_out, info_out,
           weights, beams16, looked16, wind, grad0, grad1, spread0, spread1, push,
           block_ref, count_ref, codes_out, codes_in, out1, in1, out2, in2, out3, in3, out4, in4, out5, in5,
           info, pick, place, field, beams32, looked32, rays, looked, misfit0, held, edges_out, edges_in,
           send_sems, recv_sems, halo_send, halo_recv, local_sems):
    n_radar, n_tile, total_cells, total_gates = sizes
    n = n_radar * n_tile
    nx, nz, ny = wind.shape[1] - 2, wind.shape[2], wind.shape[3]
    half = nx * nz
    group = min(16, n // 2)
    r, t = lax.axis_index("radar"), lax.axis_index("tile")
    me = r * n_tile + t
    other = jnp.where(me + 1 >= n, me + 1 - n, me + 1)

    load_bg = pltpu.make_async_copy(bg_hbm, wind.at[:, pl.ds(1, nx)], local_sems.at[0])
    load_interp = pltpu.make_async_copy(interp_hbm, weights, local_sems.at[1])
    load_blocks = pltpu.make_async_copy(block_hbm, block_ref, local_sems.at[4])
    load_counts = pltpu.make_async_copy(count_hbm, count_ref, local_sems.at[5])
    load_beams = pltpu.make_async_copy(beam_hbm, beams16, local_sems.at[2])
    load_looked = pltpu.make_async_copy(looked_hbm, looked16, local_sems.at[3])
    load_blocks.start()
    load_counts.start()
    load_bg.start()
    load_beams.start()
    load_looked.start()
    load_interp.start()

    cores, ys, zs = torus
    xs = n_radar // cores
    rounds, turns = xs * ys, zs * cores

    def distance(i, size):
        if size == 1:
            return 0
        return jnp.where(i == size - 1, 0, jnp.where(i == 0, size // 2, i + lax.div(i, 2)))

    def round_base(i, sign):
        a, b = distance(lax.div(i, ys), xs), distance(lax.rem(i, ys), ys)
        x = lax.rem(lax.div(r, cores) + xs + sign * a, xs)
        y = lax.rem(lax.div(t, zs) + ys + sign * b, ys)
        return x * (cores * n_tile) + y * zs

    hops = sorted([(c, e) for c in range(zs) for e in range(cores)], key=lambda s: -min(s[0], zs - s[0]) - 0.5 * s[1])
    turn_base = {
        sign: [lax.rem(t + zs + sign * c, zs) + lax.rem(r + cores + sign * e, cores) * n_tile for c, e in hops]
        for sign in (1, -1)}

    def for_others(action):
        def one_round(i, carry):
            base = round_base(i, 1)
            for j in range(turns):
                action(i * turns + j, base + turn_base[1][j])
            return carry

        lax.fori_loop(0, rounds - 1, one_round, 0)
        base = round_base(rounds - 1, 1)
        for j in range(turns - 1):
            action((rounds - 1) * turns + j, base + turn_base[1][j])

    barrier = pltpu.get_barrier_semaphore()

    for_others(lambda k, d: pl.semaphore_signal(barrier, inc=1, device_id=d, device_id_type=LOGICAL))

    def over_planes(count, body, carry, at_once=2):
        def some(i, carry):
            stores = []
            for u in range(at_once):
                new, carry = body(i * at_once + u, carry)
                stores += new
            for ref, index, value in stores:
                ref[index] = value
            return carry

        return lax.fori_loop(0, count // at_once, some, carry)

    lane = iota((nz, LANES), 1)

    def pack_edges(stage, source, comps, one_field):
        def plane(x, carry):
            low, high = carry
            for k in range(comps):
                if one_field:
                    a, b = source[x + 1, :, :LANES], source[x + 1, :, ny - LANES :]
                else:
                    a, b = source[k, x + 1, :, :LANES], source[k, x + 1, :, ny - LANES :]
                to = 8 * x + k
                a = pltpu.roll(a, to, 1)
                b = pltpu.roll(b, to + 1, 1)
                low = jnp.where(lane == to, a, low)
                high = jnp.where(lane == to, b, high)
            return [], (low, high)

        zero = jnp.zeros((nz, LANES), F32)
        low, high = over_planes(nx, plane, (zero, zero), 4)
        edges_out[stage, 0] = low
        edges_out[stage, 1] = high

    def chosen_planes(array, x, part):
        if part == "one":
            return array.at[x]
        return array.at[{"all": pl.ds(0, 3), "first": pl.ds(0, 1), "rest": pl.ds(1, 2)}[part], x]

    def halo_copies(stage, array, part):
        def make(i, src, dst, device):
            return pltpu.make_async_remote_copy(
                src_ref=src, dst_ref=dst,
                send_sem=halo_send.at[stage, i], recv_sem=halo_recv.at[stage, i],
                device_id=device, device_id_type=LOGICAL)

        up_t = jnp.where(t < n_tile - 1, me + 1, me - 1)
        down_t = jnp.where(t > 0, me - 1, me + 1)
        up_r = jnp.where(r < n_radar - 1, me + n_tile, me - n_tile)
        down_r = jnp.where(r > 0, me - n_tile, me + n_tile)
        planes = functools.partial(chosen_planes, array, part=part)
        copies = [
            (t < n_tile - 1, t > 0, make(0, planes(nx), planes(0), up_t)),
            (t > 0, t < n_tile - 1, make(1, planes(1), planes(nx + 1), down_t)),
        ]
        if part != "rest":
            copies += [
                (r < n_radar - 1, r > 0, make(2, edges_out.at[stage, 1], edges_in.at[stage, 0], up_r)),
                (r > 0, r < n_radar - 1, make(3, edges_out.at[stage, 0], edges_in.at[stage, 1], down_r)),
            ]
        return copies

    def send_halos(stage, array, part="all"):
        for i, (sends, receives, copy) in enumerate(halo_copies(stage, array, part)):
            pl.when(sends)(copy.start)

            @pl.when(jnp.logical_not(receives))
            def _():
                if i >= 2:
                    edges_in[stage, i - 2] = jnp.zeros((nz, LANES), F32)
                else:
                    plane = chosen_planes(array, (nx + 1) * i, part)
                    plane[...] = jnp.zeros(plane.shape, F32)

    def await_halos(stage, array, part="all"):
        for sends, receives, copy in halo_copies(stage, array, part):
            pl.when(sends)(copy.wait_send)
            pl.when(receives)(copy.wait_recv)

    def used(stage, ref, span):
        return ref.at[span, pl.ds(0, 6)] if stage in (1, 2, 4) else ref.at[span]

    def exchange_copy(stage, src, dst, d, part):
        return pltpu.make_async_remote_copy(
            src_ref=used(stage, src, d), dst_ref=used(stage, dst, me),
            send_sem=send_sems.at[stage], recv_sem=recv_sems.at[stage, part],
            device_id=d, device_id_type=LOGICAL)

    def send_all(stage, src, dst, parts):
        for_others(lambda k, d: exchange_copy(stage, src, dst, d, k // group if parts else 0).start())
        dst[me] = src[me]

    def whole(stage, src, dst, part=0, count=n - 1):
        return pltpu.make_async_remote_copy(
            src_ref=used(stage, src, pl.ds(0, count)), dst_ref=used(stage, dst, pl.ds(0, count)),
            send_sem=send_sems.at[stage], recv_sem=recv_sems.at[stage, part],
            device_id=other, device_id_type=LOGICAL)

    diff_y, diff_z = differences(nz, ny)

    def divergence(stage, source, out):
        low, high = edges_in[stage, 0], edges_in[stage, 1]

        def plane(x, total):
            s = (0.5 * (source[0, x + 2] - source[0, x]) + diff_y(source[1, x + 1], low, high, x, 1)
                 + diff_z(source[2, x + 1]))
            return [(out, x + 1, s)], total + s * s

        return over_planes(nx, plane, jnp.zeros((nz, ny), F32))

    def pushes(stage, source, x, low, high):
        v = source[x + 1]
        return (0.5 * (source[x] - source[x + 2]), -diff_y(v, low, high, x, 0), -diff_z(v))

    def total_of(v):
        return jnp.sum(jnp.sum(v, axis=0, keepdims=True), axis=1, keepdims=True)

    def to_field(source):
        for h in range(ny // LANES):
            for k in range(3):
                v = source[k, 1 : nx + 1, :, h * LANES : (h + 1) * LANES]
                field[h * half : (h + 1) * half, k * LANES : (k + 1) * LANES] = v.reshape(half, LANES).astype(BF16)

    def gather(out, extra):
        chosen = jnp.dot(pick[...], field[...], preferred_element_type=F32)
        zero = jnp.zeros((n, LANES), F32)
        rows = []
        for k in range(2):
            for c in range(3):
                rows.append(chosen[k * n : (k + 1) * n, c * LANES : (c + 1) * LANES])
        rows += [zero if extra is None else jnp.broadcast_to(extra, (n, LANES)), zero]
        out[...] = jnp.swapaxes(jnp.stack(rows, 0), 0, 1).astype(BF16)

    def observe(source, out, dst, stage, step):
        count = n // group

        def members(q):
            bases = [round_base(q * (group // turns) + i, -1) for i in range(group // turns)]
            return [base + j for base in bases for j in turn_base[-1]]

        def weights_of(d):
            return weights[pl.ds(2 * d, 2)].reshape(2 * LANES, LANES)

        def project(ds):
            return [
                lax.dot_general(source[d], weights_of(d), (((1,), (1,)), ((), ())), preferred_element_type=F32)
                for d in ds]

        def adjoints(ds, projected, cost):
            beams = [rays[d] for d in ds]
            radial = [jnp.sum(b * p, axis=0, keepdims=True) for b, p in zip(beams, projected)]
            if step is None:
                misfit = [x - looked[d] for d, x in zip(ds, radial)]
                for d, x in zip(ds, misfit):
                    misfit0[d] = x
            else:
                misfit = [misfit0[d] - step * x for d, x in zip(ds, radial)]
            for x in misfit:
                cost = cost + x * x
            for u, (b, x) in enumerate(zip(beams, misfit)):
                held[u] = (b * x).astype(BF16)
            return cost

        def back(ds):
            return [jnp.dot(held[u], weights_of(d), preferred_element_type=F32) for u, d in enumerate(ds)]

        def send(ds, values, last):
            for d, x in zip(ds, values):
                out[d] = x.astype(BF16)
            for u, d in enumerate(ds):
                if last and u == group - 1:
                    dst[me] = out[me]
                else:
                    exchange_copy(stage, out, dst, d, 0).start()

        def arrive(q, last):
            if step is None:
                whole(stage - 1, out, source, q, group - last).wait_recv()

        def middle(q, cost, last=False):
            ds, ahead = members(q), members(q + 1)
            arrive(q + 1, last)
            values = back(ds)
            projected = project(ahead)
            send(ds, values, False)
            return adjoints(ahead, projected, cost)

        arrive(0, 0)
        first = members(0)
        cost = adjoints(first, project(first), jnp.zeros((1, 2 * LANES), F32))
        cost = lax.fori_loop(0, count - 2, middle, cost)
        cost = middle(count - 2, cost, True)
        final = members(count - 1)
        send(final, back(final), True)
        return 0.5 * jnp.sum(cost, axis=1, keepdims=True)

    def scatter(source, out, to_field):
        rows = jnp.swapaxes(source[...].astype(F32), 0, 1).astype(BF16)
        landed = jnp.concatenate(
            [jnp.concatenate([rows[3 * k + c] for c in range(3)], 1) for k in range(2)], 0)
        total = jnp.zeros((nz, LANES), F32)
        for h in range(ny // LANES):
            added = jnp.dot(place[h * half : (h + 1) * half], landed, preferred_element_type=F32)
            for c in range(3):
                lanes = slice(h * LANES, (h + 1) * LANES)
                v = added[:, c * LANES : (c + 1) * LANES].reshape(nx, nz, LANES) + push[c, :, :, lanes]
                out[c, 1 : nx + 1, :, lanes] = v
                total = total + jnp.sum(v * v, axis=0)
                if to_field:
                    field[h * half : (h + 1) * half, c * LANES : (c + 1) * LANES] = v.reshape(half, LANES).astype(BF16)
        return total_of(total)

    ahead = iota((1, LANES), 1) < LANES // 2

    def code_rows(q, carry):
        ds = [q * 8 + u for u in range(8)]
        counts = [count_ref[0, d] for d in ds]
        blocks = [[block_ref[0, 2 * d + k] for k in range(2)] for d in ds]
        rows = []
        for count, pair in zip(counts, blocks):
            codes = [lax.rem(b, ny // LANES) * half + lax.div(b, ny // LANES) for b in pair]
            codes = [jnp.where(k < count, c, -1) for k, c in enumerate(codes)]
            rows.append(jnp.where(ahead, codes[0], codes[1]))
        for d, row in zip(ds, rows):
            codes_out[d] = row
        return carry

    in1[:, 6:, :] = jnp.zeros((n, 2, LANES), BF16)
    load_blocks.wait()
    load_counts.wait()
    lax.fori_loop(0, n // 8, code_rows, 0)
    load_bg.wait()
    pack_edges(BACK, wind, 3, False)
    pl.semaphore_wait(barrier, n - 1)
    send_all(0, codes_out, codes_in, False)
    send_halos(BACK, wind)
    to_field(wind)

    load_beams.wait()
    load_looked.wait()
    beams32[...] = beams16[...].astype(F32)
    looked32[...] = looked16[...].astype(F32)
    zero = jnp.zeros((n, LANES), F32)
    rows = []
    for k in range(2):
        rows += [beams32[c, pl.ds(k, n, stride=2), :] for c in range(3)]
    rows += [zero, zero]
    out_row = jnp.swapaxes(jnp.stack(rows, 0), 0, 1)
    rays[:, :, :LANES] = out_row
    eight = iota((8, LANES), 0)

    def ray_rows(q, carry):
        ds = [q * 8 + u for u in range(8)]
        counts = [count_ref[0, d] for d in ds]
        values = [rays[d, :, :LANES] for d in ds]
        seen = [[looked32[pl.ds(2 * d + k, 1), :] for k in range(2)] for d in ds]
        for d, count, v, s in zip(ds, counts, values, seen):
            rays[d, :, :LANES] = jnp.where((eight < 3) & (count > 0), v, 0.0)
            rays[d, :, LANES:] = jnp.where((eight >= 3) & (count > 1), v, 0.0)
            looked[d] = jnp.concatenate([jnp.where(count > k, s[k], 0.0) for k in range(2)], 1)
        return carry

    lax.fori_loop(0, n // 8, ray_rows, 0)

    whole(0, codes_out, codes_in).wait_recv()
    codes = codes_in[...].reshape(n, LANES)
    turned = pltpu.roll(codes, LANES // 2, 1)
    front = iota((n, LANES), 1) < LANES // 2
    code = (jnp.where(front, codes, turned), jnp.where(front, turned, codes))
    for k in range(2):
        for j in range(pick.shape[1] // LANES):
            hit = code[k] == iota((n, LANES), 1) + j * LANES
            pick[k * n : (k + 1) * n, j * LANES : (j + 1) * LANES] = jnp.where(hit, 1.0, 0.0).astype(BF16)

    gather(out1, None)
    send_all(1, out1, in1, True)
    for k in range(2):
        across = jnp.transpose(code[k])
        for j in range(pick.shape[1] // LANES):
            hit = across == iota((LANES, n), 0) + j * LANES
            place[j * LANES : (j + 1) * LANES, k * n : (k + 1) * n] = jnp.where(hit, 1.0, 0.0).astype(BF16)
    await_halos(BACK, wind)
    spread_cost0 = 0.5 * DIVERGENCE_WEIGHT * total_of(divergence(BACK, wind, spread0))
    pack_edges(SPREAD0, spread0, 1, True)
    send_halos(SPREAD0, spread0, "one")
    load_interp.wait()
    cost0 = observe(in1, out2, in2, 2, None) + spread_cost0
    await_halos(SPREAD0, spread0, "one")
    low, high = edges_in[SPREAD0, 0], edges_in[SPREAD0, 1]

    def push_plane(x, carry):
        values = pushes(SPREAD0, spread0, x, low, high)
        return [(push, (c, x), DIVERGENCE_WEIGHT * v) for c, v in enumerate(values)], carry

    over_planes(nx, push_plane, 0)
    whole(2, out2, in2).wait_recv()
    squares = scatter(in2, grad0, True)

    first = squares.astype(BF16)
    rest = squares - first.astype(F32)
    second = rest.astype(BF16)
    third = (rest - second.astype(F32)).astype(BF16)
    at = iota((1, LANES), 1)
    extra = jnp.where(at == 0, first.astype(F32), jnp.where(at == 1, second.astype(F32), jnp.where(at == 2, third.astype(F32), 0.0)))
    gather(out3, extra)
    pack_edges(GRAD0, grad0, 3, False)
    send_halos(GRAD0, grad0, "first")
    send_all(3, out3, in3, False)
    await_halos(GRAD0, grad0, "first")
    divergence(GRAD0, grad0, spread1)
    pack_edges(SPREAD1, spread1, 1, True)
    send_halos(SPREAD1, spread1, "one")
    whole(3, out3, in3).wait_recv()
    squares = jnp.sum(jnp.sum(in3[...].astype(F32), axis=0)[6:7], axis=1, keepdims=True)
    step0 = STEP_LENGTH / jnp.sqrt(squares / total_cells + EPSILON)
    cost1 = observe(in3, out4, in4, 4, step0)

    def wind_plane(x, carry):
        return [(wind, (c, x), wind[c, x] - step0 * grad0[c, x]) for c in range(3)], carry

    send_halos(REST0, grad0, "rest")
    await_halos(SPREAD1, spread1, "one")
    low1, high1 = edges_in[SPREAD1, 0], edges_in[SPREAD1, 1]

    def update_plane(x, carry):
        offsets, spreads = carry
        stores = []
        for c, v in enumerate(pushes(SPREAD1, spread1, x, low1, high1)):
            offset = -step0 * grad0[c, x + 1]
            offsets = offsets + offset * offset
            stores.append((push, (c, x), push[c, x] - step0 * (DIVERGENCE_WEIGHT * v) + BACKGROUND_WEIGHT * offset))
        spread = spread0[x + 1] - step0 * spread1[x + 1]
        return stores, (offsets, spreads + spread * spread)

    zero = jnp.zeros((nz, ny), F32)
    offsets, spreads = over_planes(nx, update_plane, (zero, zero))
    cost1 = cost1 + 0.5 * total_of(BACKGROUND_WEIGHT * offsets + DIVERGENCE_WEIGHT * spreads)
    whole(4, out4, in4).wait_recv()
    squares = scatter(in4, grad1, False)

    inner = pl.ds(1, nx)
    save_grad = pltpu.make_async_copy(grad1.at[:, inner], grad_out.at[:, inner], local_sems.at[7])
    summary = jnp.where(at == 0, squares, jnp.where(at == 1, cost0, jnp.where(at == 2, cost1, 0.0)))

    out5[...] = summary

    for_others(lambda k, d: pltpu.make_async_remote_copy(
        src_ref=out5, dst_ref=in5.at[me], send_sem=send_sems.at[5], recv_sem=recv_sems.at[5, 0],
        device_id=d, device_id_type=LOGICAL).start())
    in5[me] = summary
    save_grad.start()
    pack_edges(GRAD1, grad1, 3, False)
    send_halos(GRAD1, grad1)
    await_halos(REST0, grad0, "rest")
    over_planes(nx + 2, wind_plane, 0)
    save_wind = pltpu.make_async_copy(wind, wind_out, local_sems.at[6])
    save_wind.start()
    for i in range(2):
        info[i] = edges_in[BACK, i] - step0 * edges_in[GRAD0, i]
    info[4] = jnp.zeros((nz, LANES), F32)
    await_halos(GRAD1, grad1)
    for i in range(2):
        info[2 + i] = edges_in[GRAD1, i]
    save_edges = [
        pltpu.make_async_copy(grad1.at[:, x], grad_out.at[:, x], local_sems.at[9 + i])
        for i, x in enumerate((0, nx + 1))]
    for copy in save_edges:
        copy.start()
    whole(5, in5, in5).wait_recv()
    sums = jnp.sum(in5[...], axis=0)
    squares = jnp.sum(jnp.where(at == 0, sums, 0.0), axis=1, keepdims=True)
    step1 = STEP_LENGTH / jnp.sqrt(squares / total_cells + EPSILON)
    info[4, 0:1, :] = jnp.where(at == 0, step1, sums / total_gates)
    save_info = pltpu.make_async_copy(info, info_out, local_sems.at[8])
    save_info.start()
    save_info.wait()
    for copy in save_edges:
        copy.wait()
    save_grad.wait()
    save_wind.wait()

    pairs = ((codes_out, codes_in), (out1, in1), (out2, in2), (out3, in3), (out4, in4), (in5, in5))
    for stage, (src, dst) in enumerate(pairs):
        whole(stage, src, dst).wait_send()


def strain_kernel(wind_hbm, grad_hbm, info_hbm, final_hbm, strain_hbm, trace_ref,
                  wind, grad, info, strain, wind_sems, grad_sems, info_sem, final_sems, strain_sems):
    nx, nz, ny = wind.shape[1] - 2, wind.shape[2], wind.shape[3]
    diff_y, diff_z = differences(nz, ny)
    load_info = pltpu.make_async_copy(info_hbm, info, info_sem)
    load_info.start()
    starts = list(range(0, nx + 2, 4))
    loads = []
    for i, start in enumerate(starts):
        span = pl.ds(start, min(4, nx + 2 - start))
        loads.append((
            pltpu.make_async_copy(wind_hbm.at[:, span], wind.at[:, span], wind_sems.at[i]),
            pltpu.make_async_copy(grad_hbm.at[:, span], grad.at[:, span], grad_sems.at[i])))
        for copy in loads[-1]:
            copy.start()
    load_info.wait()
    step = info[4, 0:1, 0:1]
    low, high = (info[i] - step * info[2 + i] for i in range(2))
    scalars = info[4, 0:1, :]
    at = iota((1, LANES), 1)
    for i in range(2):
        trace_ref[i] = jnp.sum(jnp.where(at == i + 1, scalars, 0.0))

    ready, saves = 0, []
    for j in range(nx // 2):
        while ready < len(starts) and starts[ready] <= 2 * j + 3:
            for copy in loads[ready]:
                copy.wait()
            for x in range(starts[ready], min(starts[ready] + 4, nx + 2)):
                new = [wind[c, x] - step * grad[c, x] for c in range(3)]
                for c in range(3):
                    wind[c, x] = new[c]
            ready += 1
        stores = []
        for x in (2 * j, 2 * j + 1):
            v = [wind[c, x + 1] for c in range(3)]
            dx = [0.5 * (wind[c, x + 2] - wind[c, x]) for c in range(3)]
            dy = [diff_y(v[c], low, high, x, c) for c in range(3)]
            dz = [diff_z(v[c]) for c in range(3)]
            values = (dx[0], dy[1], dz[2], 0.5 * (dy[0] + dx[1]), 0.5 * (dz[0] + dx[2]), 0.5 * (dz[1] + dy[2]))
            stores += [(c, x, value) for c, value in enumerate(values)]
        for c, x, value in stores:
            strain[c, x] = value
        pair = pl.ds(2 * j, 2)
        saves += [
            pltpu.make_async_copy(wind.at[:, pl.ds(2 * j + 1, 2)], final_hbm.at[:, pair], final_sems.at[j]),
            pltpu.make_async_copy(strain.at[:, pair], strain_hbm.at[:, pair], strain_sems.at[j])]
        for copy in saves[-2:]:
            copy.start()
    for copy in saves:
        copy.wait()


def shards(n_radar, n_tile, background, interp, beam, observed, cell_block, sweep_count):
    n = n_radar * n_tile
    _, nx, nz, ny = background.shape
    slots = interp.shape[0] // n
    gate = interp.shape[1]
    blocks = nx * nz * ny // gate
    total_cells = 3 * nx * nz * ny * n
    total_gates = interp.shape[0] * n * gate
    sizes = (n_radar, n_tile, total_cells, total_gates)
    torus = (2, n_tile // 4, 4)

    smem = pl.BlockSpec(memory_space=pltpu.SMEM)
    hbm = pl.BlockSpec(memory_space=pltpu.HBM)
    message = pltpu.VMEM((n, 8, LANES), BF16)
    row = pltpu.VMEM((n, 1, LANES), F32)
    code_row = pltpu.VMEM((n, 1, LANES), jnp.int32)
    padded = pltpu.VMEM((3, nx + 2, nz, ny), F32)
    single = pltpu.VMEM((nx + 2, nz, ny), F32)
    rays = jnp.transpose(beam, (1, 0, 2))
    groups = n // min(16, n // 2)
    wind, grad, info = pl.pallas_call(
        functools.partial(kernel, sizes, torus),
        name="wind_analysis",
        out_shape=(
            jax.ShapeDtypeStruct((3, nx + 2, nz, ny), F32),
            jax.ShapeDtypeStruct((3, nx + 2, nz, ny), F32),
            jax.ShapeDtypeStruct((5, nz, LANES), F32),
        ),
        in_specs=[hbm] * 6,
        out_specs=(hbm, hbm, hbm),
        scratch_shapes=[
            pltpu.VMEM(interp.shape, BF16),
            pltpu.VMEM(rays.shape, BF16),
            pltpu.VMEM(observed.shape, BF16),
            padded, padded, padded, single, single,
            pltpu.VMEM((3, nx, nz, ny), F32),
            pltpu.SMEM((1, n * slots), jnp.int32), pltpu.SMEM((1, n), jnp.int32),
            code_row, code_row, message, message, message, message, message, message, message, message, pltpu.VMEM((1, LANES), F32), row,
            pltpu.VMEM((5, nz, LANES), F32),
            pltpu.VMEM((slots * n, blocks), BF16),
            pltpu.VMEM((blocks, slots * n), BF16),
            pltpu.VMEM((blocks, 3 * LANES), BF16),
            pltpu.VMEM(rays.shape, F32),
            pltpu.VMEM(observed.shape, F32),
            pltpu.VMEM((n, 8, slots * gate), F32),
            pltpu.VMEM((n, 1, slots * gate), F32),
            pltpu.VMEM((n, 1, slots * gate), F32),
            pltpu.VMEM((n // groups, 8, slots * gate), BF16),
            pltpu.VMEM((5, 2, nz, LANES), F32),
            pltpu.VMEM((5, 2, nz, LANES), F32),
            pltpu.SemaphoreType.DMA((6,)),
            pltpu.SemaphoreType.DMA((6, groups)),
            pltpu.SemaphoreType.DMA((6, 4)),
            pltpu.SemaphoreType.DMA((6, 4)),
            pltpu.SemaphoreType.DMA((11,)),
        ],
        compiler_params=pltpu.CompilerParams(
            collective_id=0, has_side_effects=True, vmem_limit_bytes=60 * 2**20),
    )(cell_block.reshape(1, n * slots), sweep_count, background, interp, rays, observed)

    spans = len(range(0, nx + 2, 4))
    return pl.pallas_call(
        strain_kernel,
        name="strain",
        out_shape=(
            jax.ShapeDtypeStruct(background.shape, F32),
            jax.ShapeDtypeStruct((6, nx, nz, ny), F32),
            jax.ShapeDtypeStruct((2,), F32),
        ),
        in_specs=[hbm] * 3,
        out_specs=(hbm, hbm, smem),
        scratch_shapes=[
            padded, padded, pltpu.VMEM((5, nz, LANES), F32), pltpu.VMEM((6, nx, nz, ny), F32),
            pltpu.SemaphoreType.DMA((spans,)), pltpu.SemaphoreType.DMA((spans,)), pltpu.SemaphoreType.DMA,
            pltpu.SemaphoreType.DMA((nx // 2,)), pltpu.SemaphoreType.DMA((nx // 2,))],
        compiler_params=pltpu.CompilerParams(vmem_limit_bytes=60 * 2**20),
    )(wind, grad, info)


def solution(mesh):
    n_radar, n_tile = mesh.shape["radar"], mesh.shape["tile"]
    both = ("radar", "tile")
    in_specs = (
        P(None, "tile", None, "radar"), P(both, None, None), P(both, None, None),
        P(both, None), P(both), P(both, None))
    out_specs = (P(None, "tile", None, "radar"), P(None, "tile", None, "radar"), P())
    return jax.shard_map(
        functools.partial(shards, n_radar, n_tile), mesh=mesh, in_specs=in_specs, out_specs=out_specs, check_vma=False)
```

```python
import functools

import jax
import jax.numpy as jnp
from jax import lax
from jax.experimental import pallas as pl
from jax.experimental.pallas import tpu as pltpu
from jax.sharding import PartitionSpec as P

BACKGROUND_WEIGHT = 0.5
DIVERGENCE_WEIGHT = 1.0
STEP_LENGTH = 0.3
EPSILON = 1e-06
LANES = 128
F32 = jnp.float32
BF16 = jnp.bfloat16
LOGICAL = pl.DeviceIdType.LOGICAL
BACK, SPREAD0, GRAD0, SPREAD1, GRAD1, REST0 = range(6)


def iota(shape, dim):
    return lax.broadcasted_iota(jnp.int32, shape, dim)


def differences(nz, ny):
    sub = iota((nz, ny), 0)
    wide = iota((nz, ny), 1)

    def diff_z(v):
        up = jnp.where(sub == nz - 1, 0.0, pltpu.roll(v, nz - 1, 0))
        down = jnp.where(sub == 0, 0.0, pltpu.roll(v, 1, 0))
        return 0.5 * (up - down)

    def diff_y(v, low, high, x, k):
        at = 8 * x + k
        low = pltpu.roll(low, (LANES - at) % LANES if isinstance(at, int) else lax.rem(LANES - at, LANES), 1)
        high = pltpu.roll(high, LANES - 1 - at, 1)
        up = jnp.where(wide == ny - 1, jnp.concatenate([high] * (ny // LANES), 1), pltpu.roll(v, ny - 1, 1))
        down = jnp.where(wide == 0, jnp.concatenate([low] * (ny // LANES), 1), pltpu.roll(v, 1, 1))
        return 0.5 * (up - down)

    return diff_y, diff_z


def kernel(sizes, torus, block_hbm, count_hbm, bg_hbm, interp_hbm, beam_hbm, looked_hbm,
           wind_out, grad_out, info_out,
           weights, beams16, looked16, wind, grad0, grad1, spread0, spread1, push,
           block_ref, count_ref, codes_out, codes_in, out1, in1, out2, in2, out3, in3, out4, in4, out5, in5,
           info, pick, place, field, beams32, looked32, rays, looked, misfit0, held, edges_out, edges_in,
           send_sems, recv_sems, halo_send, halo_recv, local_sems):
    n_radar, n_tile, total_cells, total_gates = sizes
    n = n_radar * n_tile
    nx, nz, ny = wind.shape[1] - 2, wind.shape[2], wind.shape[3]
    half = nx * nz
    group = min(16, n // 2)
    r, t = lax.axis_index("radar"), lax.axis_index("tile")
    me = r * n_tile + t
    other = jnp.where(me + 1 >= n, me + 1 - n, me + 1)

    load_bg = pltpu.make_async_copy(bg_hbm, wind.at[:, pl.ds(1, nx)], local_sems.at[0])
    load_interp = pltpu.make_async_copy(interp_hbm, weights, local_sems.at[1])
    load_blocks = pltpu.make_async_copy(block_hbm, block_ref, local_sems.at[4])
    load_counts = pltpu.make_async_copy(count_hbm, count_ref, local_sems.at[5])
    load_beams = pltpu.make_async_copy(beam_hbm, beams16, local_sems.at[2])
    load_looked = pltpu.make_async_copy(looked_hbm, looked16, local_sems.at[3])
    load_blocks.start()
    load_counts.start()
    load_bg.start()
    load_beams.start()
    load_looked.start()
    load_interp.start()

    cores, ys, zs = torus
    xs = n_radar // cores
    turns = zs * cores

    def distance(i, size):
        if size == 1:
            return 0
        return jnp.where(i == size - 1, 0, jnp.where(i == 0, size // 2, i + lax.div(i, 2)))

    def round_base(i):
        a, b = distance(lax.div(i, ys), xs), distance(lax.rem(i, ys), ys)
        x = lax.rem(lax.div(r, cores) + a, xs)
        y = lax.rem(lax.div(t, zs) + b, ys)
        return x * (cores * n_tile) + y * zs

    hops = sorted([(c, e) for c in range(zs) for e in range(cores)], key=lambda s: -min(s[0], zs - s[0]) - 0.5 * s[1])
    turn_base = [lax.rem(t + c, zs) + lax.rem(r + e, cores) * n_tile for c, e in hops]
    x_base = [lax.rem(lax.div(r, cores) + i, xs) * (cores * n_tile) for i in range(xs)]
    y_base = [lax.rem(lax.div(t, zs) + i, ys) * zs for i in range(ys)]
    z_base = [lax.rem(t + i, zs) for i in range(zs)]
    core_base = [lax.rem(r + i, cores) * n_tile for i in range(cores)]
    trips = [(a, b, c, e) for a in range(xs) for b in range(ys) for c in range(zs) for e in range(cores)]
    trips.sort(key=lambda s: -min(s[0], xs - s[0]) - min(s[1], ys - s[1]) - min(s[2], zs - s[2]) - 0.5 * s[3])

    def for_others(action):
        for a, b, c, e in trips[:-1]:
            action(x_base[a] + y_base[b] + z_base[c] + core_base[e])

    barrier = pltpu.get_barrier_semaphore()

    for_others(lambda d: pl.semaphore_signal(barrier, inc=1, device_id=d, device_id_type=LOGICAL))

    def over_planes(count, body, carry, at_once=2):
        def some(i, carry):
            stores = []
            for u in range(at_once):
                new, carry = body(i * at_once + u, carry)
                stores += new
            for ref, index, value in stores:
                ref[index] = value
            return carry

        return lax.fori_loop(0, count // at_once, some, carry)

    lane = iota((nz, LANES), 1)

    def pack_edges(stage, source, comps, one_field):
        def plane(x, carry):
            low, high = carry
            for k in range(comps):
                if one_field:
                    a, b = source[x + 1, :, :LANES], source[x + 1, :, ny - LANES :]
                else:
                    a, b = source[k, x + 1, :, :LANES], source[k, x + 1, :, ny - LANES :]
                to = 8 * x + k
                a = pltpu.roll(a, to, 1)
                b = pltpu.roll(b, to + 1, 1)
                low = jnp.where(lane == to, a, low)
                high = jnp.where(lane == to, b, high)
            return [], (low, high)

        zero = jnp.zeros((nz, LANES), F32)
        low, high = over_planes(nx, plane, (zero, zero), 4)
        edges_out[stage, 0] = low
        edges_out[stage, 1] = high

    def chosen_planes(array, x, part):
        if part == "one":
            return array.at[x]
        return array.at[{"all": pl.ds(0, 3), "first": pl.ds(0, 1), "rest": pl.ds(1, 2)}[part], x]

    def halo_copies(stage, array, part):
        def make(i, src, dst, device):
            return pltpu.make_async_remote_copy(
                src_ref=src, dst_ref=dst,
                send_sem=halo_send.at[stage, i], recv_sem=halo_recv.at[stage, i],
                device_id=device, device_id_type=LOGICAL)

        up_t = jnp.where(t < n_tile - 1, me + 1, me - 1)
        down_t = jnp.where(t > 0, me - 1, me + 1)
        up_r = jnp.where(r < n_radar - 1, me + n_tile, me - n_tile)
        down_r = jnp.where(r > 0, me - n_tile, me + n_tile)
        planes = functools.partial(chosen_planes, array, part=part)
        copies = [
            (t < n_tile - 1, t > 0, make(0, planes(nx), planes(0), up_t)),
            (t > 0, t < n_tile - 1, make(1, planes(1), planes(nx + 1), down_t)),
        ]
        if part != "rest":
            copies += [
                (r < n_radar - 1, r > 0, make(2, edges_out.at[stage, 1], edges_in.at[stage, 0], up_r)),
                (r > 0, r < n_radar - 1, make(3, edges_out.at[stage, 0], edges_in.at[stage, 1], down_r)),
            ]
        return copies

    def send_halos(stage, array, part="all"):
        for i, (sends, receives, copy) in enumerate(halo_copies(stage, array, part)):
            pl.when(sends)(copy.start)

            @pl.when(jnp.logical_not(receives))
            def _():
                if i >= 2:
                    edges_in[stage, i - 2] = jnp.zeros((nz, LANES), F32)
                else:
                    plane = chosen_planes(array, (nx + 1) * i, part)
                    plane[...] = jnp.zeros(plane.shape, F32)

    def await_halos(stage, array, part="all"):
        for sends, receives, copy in halo_copies(stage, array, part):
            pl.when(sends)(copy.wait_send)
            pl.when(receives)(copy.wait_recv)

    def used(stage, ref, span):
        return ref.at[span, pl.ds(0, 6)] if stage in (1, 2, 4) else ref.at[span]

    def exchange_copy(stage, src, dst, d):
        return pltpu.make_async_remote_copy(
            src_ref=used(stage, src, d), dst_ref=used(stage, dst, me),
            send_sem=send_sems.at[stage], recv_sem=recv_sems.at[stage],
            device_id=d, device_id_type=LOGICAL)

    def send_all(stage, src, dst):
        for_others(lambda d: exchange_copy(stage, src, dst, d).start())
        dst[me] = src[me]

    def whole(stage, src, dst):
        count = n - 1
        return pltpu.make_async_remote_copy(
            src_ref=used(stage, src, pl.ds(0, count)), dst_ref=used(stage, dst, pl.ds(0, count)),
            send_sem=send_sems.at[stage], recv_sem=recv_sems.at[stage],
            device_id=other, device_id_type=LOGICAL)

    diff_y, diff_z = differences(nz, ny)

    def divergence(stage, source, out):
        low, high = edges_in[stage, 0], edges_in[stage, 1]

        def plane(x, total):
            s = (0.5 * (source[0, x + 2] - source[0, x]) + diff_y(source[1, x + 1], low, high, x, 1)
                 + diff_z(source[2, x + 1]))
            return [(out, x + 1, s)], total + s * s

        return over_planes(nx, plane, jnp.zeros((nz, ny), F32))

    def pushes(stage, source, x, low, high):
        v = source[x + 1]
        return (0.5 * (source[x] - source[x + 2]), -diff_y(v, low, high, x, 0), -diff_z(v))

    def total_of(v):
        return jnp.sum(jnp.sum(v, axis=0, keepdims=True), axis=1, keepdims=True)

    def to_field(source):
        for h in range(ny // LANES):
            for k in range(3):
                v = source[k, 1 : nx + 1, :, h * LANES : (h + 1) * LANES]
                field[h * half : (h + 1) * half, k * LANES : (k + 1) * LANES] = v.reshape(half, LANES).astype(BF16)

    def gather(out, extra):
        chosen = jnp.dot(pick[...], field[...], preferred_element_type=F32)
        zero = jnp.zeros((n, LANES), F32)
        rows = []
        for k in range(2):
            for c in range(3):
                rows.append(chosen[k * n : (k + 1) * n, c * LANES : (c + 1) * LANES])
        rows += [zero if extra is None else jnp.broadcast_to(extra, (n, LANES)), zero]
        out[...] = jnp.swapaxes(jnp.stack(rows, 0), 0, 1).astype(BF16)

    def observe(source, out, dst, stage, step):
        count = n // group

        def members(q):
            bases = [round_base(q * (group // turns) + i) for i in range(group // turns)]
            return [base + j for base in bases for j in turn_base]

        def weights_of(d):
            return weights[pl.ds(2 * d, 2)].reshape(2 * LANES, LANES)

        def project(ds):
            return [
                lax.dot_general(source[d], weights_of(d), (((1,), (1,)), ((), ())), preferred_element_type=F32)
                for d in ds]

        def adjoints(ds, projected, cost):
            beams = [rays[d] for d in ds]
            radial = [jnp.sum(b * p, axis=0, keepdims=True) for b, p in zip(beams, projected)]
            if step is None:
                misfit = [x - looked[d] for d, x in zip(ds, radial)]
                for d, x in zip(ds, misfit):
                    misfit0[d] = x
            else:
                misfit = [misfit0[d] - step * x for d, x in zip(ds, radial)]
            for x in misfit:
                cost = cost + x * x
            for u, (b, x) in enumerate(zip(beams, misfit)):
                held[u] = (b * x).astype(BF16)
            return cost

        def back(ds):
            return [jnp.dot(held[u], weights_of(d), preferred_element_type=F32) for u, d in enumerate(ds)]

        def send(ds, values, last):
            for d, x in zip(ds, values):
                out[d] = x.astype(BF16)
            for u, d in enumerate(ds):
                if last and u == group - 1:
                    dst[me] = out[me]
                else:
                    exchange_copy(stage, out, dst, d).start()

        def middle(q, cost):
            ds, ahead = members(q), members(q + 1)
            values = back(ds)
            projected = project(ahead)
            send(ds, values, False)
            return adjoints(ahead, projected, cost)

        first = members(0)
        cost = adjoints(first, project(first), jnp.zeros((1, 2 * LANES), F32))
        cost = lax.fori_loop(0, count - 1, middle, cost)
        final = members(count - 1)
        send(final, back(final), True)
        return 0.5 * jnp.sum(cost, axis=1, keepdims=True)

    def scatter(source, out, to_field):
        rows = jnp.swapaxes(source[...].astype(F32), 0, 1).astype(BF16)
        landed = jnp.concatenate(
            [jnp.concatenate([rows[3 * k + c] for c in range(3)], 1) for k in range(2)], 0)
        total = jnp.zeros((nz, LANES), F32)
        for h in range(ny // LANES):
            added = jnp.dot(place[h * half : (h + 1) * half], landed, preferred_element_type=F32)
            for c in range(3):
                lanes = slice(h * LANES, (h + 1) * LANES)
                v = added[:, c * LANES : (c + 1) * LANES].reshape(nx, nz, LANES) + push[c, :, :, lanes]
                out[c, 1 : nx + 1, :, lanes] = v
                total = total + jnp.sum(v * v, axis=0)
                if to_field:
                    field[h * half : (h + 1) * half, c * LANES : (c + 1) * LANES] = v.reshape(half, LANES).astype(BF16)
        return total_of(total)

    ahead = iota((1, LANES), 1) < LANES // 2

    def code_rows(q, carry):
        ds = [q * 8 + u for u in range(8)]
        counts = [count_ref[0, d] for d in ds]
        blocks = [[block_ref[0, 2 * d + k] for k in range(2)] for d in ds]
        rows = []
        for count, pair in zip(counts, blocks):
            codes = [lax.rem(b, ny // LANES) * half + lax.div(b, ny // LANES) for b in pair]
            codes = [jnp.where(k < count, c, -1) for k, c in enumerate(codes)]
            rows.append(jnp.where(ahead, codes[0], codes[1]))
        for d, row in zip(ds, rows):
            codes_out[d] = row
        return carry

    in1[:, 6:, :] = jnp.zeros((n, 2, LANES), BF16)
    load_blocks.wait()
    load_counts.wait()
    lax.fori_loop(0, n // 8, code_rows, 0)
    load_bg.wait()
    pack_edges(BACK, wind, 3, False)
    pl.semaphore_wait(barrier, n - 1)
    send_all(0, codes_out, codes_in)
    send_halos(BACK, wind)
    to_field(wind)

    load_beams.wait()
    load_looked.wait()
    beams32[...] = beams16[...].astype(F32)
    looked32[...] = looked16[...].astype(F32)
    zero = jnp.zeros((n, LANES), F32)
    rows = []
    for k in range(2):
        rows += [beams32[c, pl.ds(k, n, stride=2), :] for c in range(3)]
    rows += [zero, zero]
    out_row = jnp.swapaxes(jnp.stack(rows, 0), 0, 1)
    rays[:, :, :LANES] = out_row
    eight = iota((8, LANES), 0)

    def ray_rows(q, carry):
        ds = [q * 8 + u for u in range(8)]
        counts = [count_ref[0, d] for d in ds]
        values = [rays[d, :, :LANES] for d in ds]
        seen = [[looked32[pl.ds(2 * d + k, 1), :] for k in range(2)] for d in ds]
        for d, count, v, s in zip(ds, counts, values, seen):
            rays[d, :, :LANES] = jnp.where((eight < 3) & (count > 0), v, 0.0)
            rays[d, :, LANES:] = jnp.where((eight >= 3) & (count > 1), v, 0.0)
            looked[d] = jnp.concatenate([jnp.where(count > k, s[k], 0.0) for k in range(2)], 1)
        return carry

    lax.fori_loop(0, n // 8, ray_rows, 0)

    whole(0, codes_out, codes_in).wait_recv()
    codes = codes_in[...].reshape(n, LANES)
    turned = pltpu.roll(codes, LANES // 2, 1)
    front = iota((n, LANES), 1) < LANES // 2
    code = (jnp.where(front, codes, turned), jnp.where(front, turned, codes))
    for k in range(2):
        for j in range(pick.shape[1] // LANES):
            hit = code[k] == iota((n, LANES), 1) + j * LANES
            pick[k * n : (k + 1) * n, j * LANES : (j + 1) * LANES] = jnp.where(hit, 1.0, 0.0).astype(BF16)

    gather(out1, None)
    send_all(1, out1, in1)
    for k in range(2):
        across = jnp.transpose(code[k])
        for j in range(pick.shape[1] // LANES):
            hit = across == iota((LANES, n), 0) + j * LANES
            place[j * LANES : (j + 1) * LANES, k * n : (k + 1) * n] = jnp.where(hit, 1.0, 0.0).astype(BF16)
    await_halos(BACK, wind)
    spread_cost0 = 0.5 * DIVERGENCE_WEIGHT * total_of(divergence(BACK, wind, spread0))
    pack_edges(SPREAD0, spread0, 1, True)
    send_halos(SPREAD0, spread0, "one")
    load_interp.wait()
    whole(1, out1, in1).wait_recv()
    cost0 = observe(in1, out2, in2, 2, None) + spread_cost0
    await_halos(SPREAD0, spread0, "one")
    low, high = edges_in[SPREAD0, 0], edges_in[SPREAD0, 1]

    def push_plane(x, carry):
        values = pushes(SPREAD0, spread0, x, low, high)
        return [(push, (c, x), DIVERGENCE_WEIGHT * v) for c, v in enumerate(values)], carry

    over_planes(nx, push_plane, 0)
    whole(2, out2, in2).wait_recv()
    squares = scatter(in2, grad0, True)

    first = squares.astype(BF16)
    rest = squares - first.astype(F32)
    second = rest.astype(BF16)
    third = (rest - second.astype(F32)).astype(BF16)
    at = iota((1, LANES), 1)
    extra = jnp.where(at == 0, first.astype(F32), jnp.where(at == 1, second.astype(F32), jnp.where(at == 2, third.astype(F32), 0.0)))
    gather(out3, extra)
    pack_edges(GRAD0, grad0, 3, False)
    send_halos(GRAD0, grad0, "first")
    send_all(3, out3, in3)
    await_halos(GRAD0, grad0, "first")
    divergence(GRAD0, grad0, spread1)
    pack_edges(SPREAD1, spread1, 1, True)
    send_halos(SPREAD1, spread1, "one")
    whole(3, out3, in3).wait_recv()
    squares = jnp.sum(jnp.sum(in3[...].astype(F32), axis=0)[6:7], axis=1, keepdims=True)
    step0 = STEP_LENGTH / jnp.sqrt(squares / total_cells + EPSILON)
    cost1 = observe(in3, out4, in4, 4, step0)

    def wind_plane(x, carry):
        return [(wind, (c, x), wind[c, x] - step0 * grad0[c, x]) for c in range(3)], carry

    send_halos(REST0, grad0, "rest")
    await_halos(SPREAD1, spread1, "one")
    low1, high1 = edges_in[SPREAD1, 0], edges_in[SPREAD1, 1]

    def update_plane(x, carry):
        offsets, spreads = carry
        stores = []
        for c, v in enumerate(pushes(SPREAD1, spread1, x, low1, high1)):
            offset = -step0 * grad0[c, x + 1]
            offsets = offsets + offset * offset
            stores.append((push, (c, x), push[c, x] - step0 * (DIVERGENCE_WEIGHT * v) + BACKGROUND_WEIGHT * offset))
        spread = spread0[x + 1] - step0 * spread1[x + 1]
        return stores, (offsets, spreads + spread * spread)

    zero = jnp.zeros((nz, ny), F32)
    offsets, spreads = over_planes(nx, update_plane, (zero, zero))
    cost1 = cost1 + 0.5 * total_of(BACKGROUND_WEIGHT * offsets + DIVERGENCE_WEIGHT * spreads)
    whole(4, out4, in4).wait_recv()
    squares = scatter(in4, grad1, False)

    inner = pl.ds(1, nx)
    save_grad = pltpu.make_async_copy(grad1.at[:, inner], grad_out.at[:, inner], local_sems.at[7])
    summary = jnp.where(at == 0, squares, jnp.where(at == 1, cost0, jnp.where(at == 2, cost1, 0.0)))

    out5[...] = summary

    for_others(lambda d: pltpu.make_async_remote_copy(
        src_ref=out5, dst_ref=in5.at[me], send_sem=send_sems.at[5], recv_sem=recv_sems.at[5],
        device_id=d, device_id_type=LOGICAL).start())
    in5[me] = summary
    save_grad.start()
    pack_edges(GRAD1, grad1, 3, False)
    send_halos(GRAD1, grad1)
    await_halos(REST0, grad0, "rest")
    over_planes(nx + 2, wind_plane, 0)
    save_wind = pltpu.make_async_copy(wind, wind_out, local_sems.at[6])
    save_wind.start()
    for i in range(2):
        info[i] = edges_in[BACK, i] - step0 * edges_in[GRAD0, i]
    info[4] = jnp.zeros((nz, LANES), F32)
    await_halos(GRAD1, grad1)
    for i in range(2):
        info[2 + i] = edges_in[GRAD1, i]
    save_edges = [
        pltpu.make_async_copy(grad1.at[:, x], grad_out.at[:, x], local_sems.at[9 + i])
        for i, x in enumerate((0, nx + 1))]
    for copy in save_edges:
        copy.start()
    whole(5, in5, in5).wait_recv()
    sums = jnp.sum(in5[...], axis=0)
    squares = jnp.sum(jnp.where(at == 0, sums, 0.0), axis=1, keepdims=True)
    step1 = STEP_LENGTH / jnp.sqrt(squares / total_cells + EPSILON)
    info[4, 0:1, :] = jnp.where(at == 0, step1, sums / total_gates)
    save_info = pltpu.make_async_copy(info, info_out, local_sems.at[8])
    save_info.start()
    save_info.wait()
    for copy in save_edges:
        copy.wait()
    save_grad.wait()
    save_wind.wait()

    pairs = ((codes_out, codes_in), (out1, in1), (out2, in2), (out3, in3), (out4, in4), (in5, in5))
    for stage, (src, dst) in enumerate(pairs):
        whole(stage, src, dst).wait_send()


def strain_kernel(wind_hbm, grad_hbm, info_hbm, final_hbm, strain_hbm, trace_ref,
                  wind, grad, info, strain, wind_sems, grad_sems, info_sem, final_sems, strain_sems):
    nx, nz, ny = wind.shape[1] - 2, wind.shape[2], wind.shape[3]
    diff_y, diff_z = differences(nz, ny)
    load_info = pltpu.make_async_copy(info_hbm, info, info_sem)
    load_info.start()
    starts = list(range(0, nx + 2, 4))
    loads = []
    for i, start in enumerate(starts):
        span = pl.ds(start, min(4, nx + 2 - start))
        loads.append((
            pltpu.make_async_copy(wind_hbm.at[:, span], wind.at[:, span], wind_sems.at[i]),
            pltpu.make_async_copy(grad_hbm.at[:, span], grad.at[:, span], grad_sems.at[i])))
        for copy in loads[-1]:
            copy.start()
    load_info.wait()
    step = info[4, 0:1, 0:1]
    low, high = (info[i] - step * info[2 + i] for i in range(2))
    scalars = info[4, 0:1, :]
    at = iota((1, LANES), 1)
    for i in range(2):
        trace_ref[i] = jnp.sum(jnp.where(at == i + 1, scalars, 0.0))

    ready, saves = 0, []
    for j in range(nx // 2):
        while ready < len(starts) and starts[ready] <= 2 * j + 3:
            for copy in loads[ready]:
                copy.wait()
            for x in range(starts[ready], min(starts[ready] + 4, nx + 2)):
                new = [wind[c, x] - step * grad[c, x] for c in range(3)]
                for c in range(3):
                    wind[c, x] = new[c]
            ready += 1
        stores = []
        for x in (2 * j, 2 * j + 1):
            v = [wind[c, x + 1] for c in range(3)]
            dx = [0.5 * (wind[c, x + 2] - wind[c, x]) for c in range(3)]
            dy = [diff_y(v[c], low, high, x, c) for c in range(3)]
            dz = [diff_z(v[c]) for c in range(3)]
            values = (dx[0], dy[1], dz[2], 0.5 * (dy[0] + dx[1]), 0.5 * (dz[0] + dx[2]), 0.5 * (dz[1] + dy[2]))
            stores += [(c, x, value) for c, value in enumerate(values)]
        for c, x, value in stores:
            strain[c, x] = value
        pair = pl.ds(2 * j, 2)
        saves += [
            pltpu.make_async_copy(wind.at[:, pl.ds(2 * j + 1, 2)], final_hbm.at[:, pair], final_sems.at[j]),
            pltpu.make_async_copy(strain.at[:, pair], strain_hbm.at[:, pair], strain_sems.at[j])]
        for copy in saves[-2:]:
            copy.start()
    for copy in saves:
        copy.wait()


def shards(n_radar, n_tile, background, interp, beam, observed, cell_block, sweep_count):
    n = n_radar * n_tile
    _, nx, nz, ny = background.shape
    slots = interp.shape[0] // n
    gate = interp.shape[1]
    blocks = nx * nz * ny // gate
    total_cells = 3 * nx * nz * ny * n
    total_gates = interp.shape[0] * n * gate
    sizes = (n_radar, n_tile, total_cells, total_gates)
    torus = (2, n_tile // 4, 4)

    smem = pl.BlockSpec(memory_space=pltpu.SMEM)
    hbm = pl.BlockSpec(memory_space=pltpu.HBM)
    message = pltpu.VMEM((n, 8, LANES), BF16)
    row = pltpu.VMEM((n, 1, LANES), F32)
    code_row = pltpu.VMEM((n, 1, LANES), jnp.int32)
    padded = pltpu.VMEM((3, nx + 2, nz, ny), F32)
    single = pltpu.VMEM((nx + 2, nz, ny), F32)
    rays = jnp.transpose(beam, (1, 0, 2))
    groups = n // min(16, n // 2)
    wind, grad, info = pl.pallas_call(
        functools.partial(kernel, sizes, torus),
        name="wind_analysis",
        out_shape=(
            jax.ShapeDtypeStruct((3, nx + 2, nz, ny), F32),
            jax.ShapeDtypeStruct((3, nx + 2, nz, ny), F32),
            jax.ShapeDtypeStruct((5, nz, LANES), F32),
        ),
        in_specs=[hbm] * 6,
        out_specs=(hbm, hbm, hbm),
        scratch_shapes=[
            pltpu.VMEM(interp.shape, BF16),
            pltpu.VMEM(rays.shape, BF16),
            pltpu.VMEM(observed.shape, BF16),
            padded, padded, padded, single, single,
            pltpu.VMEM((3, nx, nz, ny), F32),
            pltpu.SMEM((1, n * slots), jnp.int32), pltpu.SMEM((1, n), jnp.int32),
            code_row, code_row, message, message, message, message, message, message, message, message, pltpu.VMEM((1, LANES), F32), row,
            pltpu.VMEM((5, nz, LANES), F32),
            pltpu.VMEM((slots * n, blocks), BF16),
            pltpu.VMEM((blocks, slots * n), BF16),
            pltpu.VMEM((blocks, 3 * LANES), BF16),
            pltpu.VMEM(rays.shape, F32),
            pltpu.VMEM(observed.shape, F32),
            pltpu.VMEM((n, 8, slots * gate), F32),
            pltpu.VMEM((n, 1, slots * gate), F32),
            pltpu.VMEM((n, 1, slots * gate), F32),
            pltpu.VMEM((n // groups, 8, slots * gate), BF16),
            pltpu.VMEM((5, 2, nz, LANES), F32),
            pltpu.VMEM((5, 2, nz, LANES), F32),
            pltpu.SemaphoreType.DMA((6,)),
            pltpu.SemaphoreType.DMA((6,)),
            pltpu.SemaphoreType.DMA((6, 4)),
            pltpu.SemaphoreType.DMA((6, 4)),
            pltpu.SemaphoreType.DMA((11,)),
        ],
        compiler_params=pltpu.CompilerParams(
            collective_id=0, has_side_effects=True, vmem_limit_bytes=60 * 2**20),
    )(cell_block.reshape(1, n * slots), sweep_count, background, interp, rays, observed)

    spans = len(range(0, nx + 2, 4))
    return pl.pallas_call(
        strain_kernel,
        name="strain",
        out_shape=(
            jax.ShapeDtypeStruct(background.shape, F32),
            jax.ShapeDtypeStruct((6, nx, nz, ny), F32),
            jax.ShapeDtypeStruct((2,), F32),
        ),
        in_specs=[hbm] * 3,
        out_specs=(hbm, hbm, smem),
        scratch_shapes=[
            padded, padded, pltpu.VMEM((5, nz, LANES), F32), pltpu.VMEM((6, nx, nz, ny), F32),
            pltpu.SemaphoreType.DMA((spans,)), pltpu.SemaphoreType.DMA((spans,)), pltpu.SemaphoreType.DMA,
            pltpu.SemaphoreType.DMA((nx // 2,)), pltpu.SemaphoreType.DMA((nx // 2,))],
        compiler_params=pltpu.CompilerParams(vmem_limit_bytes=60 * 2**20),
    )(wind, grad, info)


def solution(mesh):
    n_radar, n_tile = mesh.shape["radar"], mesh.shape["tile"]
    both = ("radar", "tile")
    in_specs = (
        P(None, "tile", None, "radar"), P(both, None, None), P(both, None, None),
        P(both, None), P(both), P(both, None))
    out_specs = (P(None, "tile", None, "radar"), P(None, "tile", None, "radar"), P())
    return jax.shard_map(
        functools.partial(shards, n_radar, n_tile), mesh=mesh, in_specs=in_specs, out_specs=out_specs, check_vma=False)
```

```python
import functools

import jax
import jax.numpy as jnp
from jax import lax
from jax.experimental import pallas as pl
from jax.experimental.pallas import tpu as pltpu
from jax.sharding import PartitionSpec as P

BACKGROUND_WEIGHT = 0.5
DIVERGENCE_WEIGHT = 1.0
STEP_LENGTH = 0.3
EPSILON = 1e-06
LANES = 128
F32 = jnp.float32
BF16 = jnp.bfloat16
LOGICAL = pl.DeviceIdType.LOGICAL
BACK, SPREAD0, GRAD0, SPREAD1, GRAD1, REST0 = range(6)


def iota(shape, dim):
    return lax.broadcasted_iota(jnp.int32, shape, dim)


def differences(nz, ny):
    sub = iota((nz, ny), 0)
    wide = iota((nz, ny), 1)

    def diff_z(v):
        up = jnp.where(sub == nz - 1, 0.0, pltpu.roll(v, nz - 1, 0))
        down = jnp.where(sub == 0, 0.0, pltpu.roll(v, 1, 0))
        return 0.5 * (up - down)

    def diff_y(v, low, high, x, k):
        at = 8 * x + k
        low = pltpu.roll(low, (LANES - at) % LANES if isinstance(at, int) else lax.rem(LANES - at, LANES), 1)
        high = pltpu.roll(high, LANES - 1 - at, 1)
        up = jnp.where(wide == ny - 1, jnp.concatenate([high] * (ny // LANES), 1), pltpu.roll(v, ny - 1, 1))
        down = jnp.where(wide == 0, jnp.concatenate([low] * (ny // LANES), 1), pltpu.roll(v, 1, 1))
        return 0.5 * (up - down)

    return diff_y, diff_z


def kernel(sizes, torus, block_hbm, count_hbm, bg_hbm, interp_hbm, beam_hbm, looked_hbm,
           wind_out, grad_out, info_out,
           weights, beams16, looked16, wind, grad0, grad1, spread0, spread1, push,
           block_ref, count_ref, codes_out, codes_in, out1, in1, out2, in2, out3, in3, out4, in4, out5, in5,
           info, pick, place, field, beams32, looked32, rays, looked, misfit0, held, edges_out, edges_in,
           send_sems, recv_sems, halo_send, halo_recv, local_sems):
    n_radar, n_tile, total_cells, total_gates = sizes
    n = n_radar * n_tile
    nx, nz, ny = wind.shape[1] - 2, wind.shape[2], wind.shape[3]
    half = nx * nz
    group = min(16, n // 2)
    r, t = lax.axis_index("radar"), lax.axis_index("tile")
    me = r * n_tile + t
    other = jnp.where(me + 1 >= n, me + 1 - n, me + 1)

    load_bg = pltpu.make_async_copy(bg_hbm, wind.at[:, pl.ds(1, nx)], local_sems.at[0])
    load_interp = pltpu.make_async_copy(interp_hbm, weights, local_sems.at[1])
    load_blocks = pltpu.make_async_copy(block_hbm, block_ref, local_sems.at[4])
    load_counts = pltpu.make_async_copy(count_hbm, count_ref, local_sems.at[5])
    load_beams = pltpu.make_async_copy(beam_hbm, beams16, local_sems.at[2])
    load_looked = pltpu.make_async_copy(looked_hbm, looked16, local_sems.at[3])
    load_blocks.start()
    load_counts.start()
    load_bg.start()
    load_beams.start()
    load_looked.start()
    load_interp.start()

    cores, ys, zs = torus
    xs = n_radar // cores
    turns = zs * cores

    def distance(i, size):
        if size == 1:
            return 0
        return jnp.where(i == size - 1, 0, jnp.where(i == 0, size // 2, i + lax.div(i, 2)))

    def round_base(i):
        a, b = distance(lax.div(i, ys), xs), distance(lax.rem(i, ys), ys)
        x = lax.rem(lax.div(r, cores) + a, xs)
        y = lax.rem(lax.div(t, zs) + b, ys)
        return x * (cores * n_tile) + y * zs

    hops = sorted([(c, e) for c in range(zs) for e in range(cores)], key=lambda s: -min(s[0], zs - s[0]) - 0.5 * s[1])
    turn_base = [lax.rem(t + c, zs) + lax.rem(r + e, cores) * n_tile for c, e in hops]
    x_base = [lax.rem(lax.div(r, cores) + i, xs) * (cores * n_tile) for i in range(xs)]
    y_base = [lax.rem(lax.div(t, zs) + i, ys) * zs for i in range(ys)]
    z_base = [lax.rem(t + i, zs) for i in range(zs)]
    core_base = [lax.rem(r + i, cores) * n_tile for i in range(cores)]
    trips = [(a, b, c, e) for a in range(xs) for b in range(ys) for c in range(zs) for e in range(cores)]
    trips.sort(key=lambda s: -min(s[0], xs - s[0]) - min(s[1], ys - s[1]) - min(s[2], zs - s[2]) - 0.5 * s[3])

    def for_others(action):
        for a, b, c, e in trips[:-1]:
            action(x_base[a] + y_base[b] + z_base[c] + core_base[e])

    barrier = pltpu.get_barrier_semaphore()

    for_others(lambda d: pl.semaphore_signal(barrier, inc=1, device_id=d, device_id_type=LOGICAL))

    def over_planes(count, body, carry, at_once=2):
        def some(i, carry):
            stores = []
            for u in range(at_once):
                new, carry = body(i * at_once + u, carry)
                stores += new
            for ref, index, value in stores:
                ref[index] = value
            return carry

        return lax.fori_loop(0, count // at_once, some, carry)

    lane = iota((nz, LANES), 1)

    def pack_edges(stage, source, comps, one_field):
        def plane(x, carry):
            low, high = carry
            for k in range(comps):
                if one_field:
                    a, b = source[x + 1, :, :LANES], source[x + 1, :, ny - LANES :]
                else:
                    a, b = source[k, x + 1, :, :LANES], source[k, x + 1, :, ny - LANES :]
                to = 8 * x + k
                a = pltpu.roll(a, to, 1)
                b = pltpu.roll(b, to + 1, 1)
                low = jnp.where(lane == to, a, low)
                high = jnp.where(lane == to, b, high)
            return [], (low, high)

        zero = jnp.zeros((nz, LANES), F32)
        low, high = over_planes(nx, plane, (zero, zero), 4)
        edges_out[stage, 0] = low
        edges_out[stage, 1] = high

    def chosen_planes(array, x, part):
        if part == "one":
            return array.at[x]
        return array.at[{"all": pl.ds(0, 3), "first": pl.ds(0, 1), "rest": pl.ds(1, 2)}[part], x]

    def halo_copies(stage, array, part):
        def make(i, src, dst, device):
            return pltpu.make_async_remote_copy(
                src_ref=src, dst_ref=dst,
                send_sem=halo_send.at[stage, i], recv_sem=halo_recv.at[stage, i],
                device_id=device, device_id_type=LOGICAL)

        up_t = jnp.where(t < n_tile - 1, me + 1, me - 1)
        down_t = jnp.where(t > 0, me - 1, me + 1)
        up_r = jnp.where(r < n_radar - 1, me + n_tile, me - n_tile)
        down_r = jnp.where(r > 0, me - n_tile, me + n_tile)
        planes = functools.partial(chosen_planes, array, part=part)
        copies = [
            (t < n_tile - 1, t > 0, make(0, planes(nx), planes(0), up_t)),
            (t > 0, t < n_tile - 1, make(1, planes(1), planes(nx + 1), down_t)),
        ]
        if part != "rest":
            copies += [
                (r < n_radar - 1, r > 0, make(2, edges_out.at[stage, 1], edges_in.at[stage, 0], up_r)),
                (r > 0, r < n_radar - 1, make(3, edges_out.at[stage, 0], edges_in.at[stage, 1], down_r)),
            ]
        return copies

    def send_halos(stage, array, part="all"):
        for i, (sends, receives, copy) in enumerate(halo_copies(stage, array, part)):
            pl.when(sends)(copy.start)

            @pl.when(jnp.logical_not(receives))
            def _():
                if i >= 2:
                    edges_in[stage, i - 2] = jnp.zeros((nz, LANES), F32)
                else:
                    plane = chosen_planes(array, (nx + 1) * i, part)
                    plane[...] = jnp.zeros(plane.shape, F32)

    def await_halos(stage, array, part="all"):
        for sends, receives, copy in halo_copies(stage, array, part):
            pl.when(sends)(copy.wait_send)
            pl.when(receives)(copy.wait_recv)

    def used(stage, ref, span):
        return ref.at[span, pl.ds(0, 6)] if stage in (1, 2, 4) else ref.at[span]

    def exchange_copy(stage, src, dst, d):
        return pltpu.make_async_remote_copy(
            src_ref=used(stage, src, d), dst_ref=used(stage, dst, me),
            send_sem=send_sems.at[stage], recv_sem=recv_sems.at[stage],
            device_id=d, device_id_type=LOGICAL)

    def send_all(stage, src, dst):
        for_others(lambda d: exchange_copy(stage, src, dst, d).start())
        dst[me] = src[me]

    def whole(stage, src, dst):
        count = n - 1
        return pltpu.make_async_remote_copy(
            src_ref=used(stage, src, pl.ds(0, count)), dst_ref=used(stage, dst, pl.ds(0, count)),
            send_sem=send_sems.at[stage], recv_sem=recv_sems.at[stage],
            device_id=other, device_id_type=LOGICAL)

    diff_y, diff_z = differences(nz, ny)

    def divergence(stage, source, out):
        low, high = edges_in[stage, 0], edges_in[stage, 1]

        def plane(x, total):
            s = (0.5 * (source[0, x + 2] - source[0, x]) + diff_y(source[1, x + 1], low, high, x, 1)
                 + diff_z(source[2, x + 1]))
            return [(out, x + 1, s)], total + s * s

        return over_planes(nx, plane, jnp.zeros((nz, ny), F32))

    def pushes(stage, source, x, low, high):
        v = source[x + 1]
        return (0.5 * (source[x] - source[x + 2]), -diff_y(v, low, high, x, 0), -diff_z(v))

    def total_of(v):
        return jnp.sum(jnp.sum(v, axis=0, keepdims=True), axis=1, keepdims=True)

    def to_field(source):
        for h in range(ny // LANES):
            for k in range(3):
                v = source[k, 1 : nx + 1, :, h * LANES : (h + 1) * LANES]
                field[h * half : (h + 1) * half, k * LANES : (k + 1) * LANES] = v.reshape(half, LANES).astype(BF16)

    def gather(out, extra):
        chosen = jnp.dot(pick[...], field[...], preferred_element_type=F32)
        zero = jnp.zeros((n, LANES), F32)
        rows = []
        for k in range(2):
            for c in range(3):
                rows.append(chosen[k * n : (k + 1) * n, c * LANES : (c + 1) * LANES])
        rows += [zero if extra is None else jnp.broadcast_to(extra, (n, LANES)), zero]
        out[...] = jnp.swapaxes(jnp.stack(rows, 0), 0, 1).astype(BF16)

    def observe(source, out, dst, stage, step):
        count = n // group

        def members(q):
            bases = [round_base(q * (group // turns) + i) for i in range(group // turns)]
            return [base + j for base in bases for j in turn_base]

        def weights_of(d):
            return weights[pl.ds(2 * d, 2)].reshape(2 * LANES, LANES)

        def project(ds):
            return [
                lax.dot_general(source[d], weights_of(d), (((1,), (1,)), ((), ())), preferred_element_type=F32)
                for d in ds]

        def adjoints(ds, projected, cost):
            beams = [rays[d] for d in ds]
            radial = [jnp.sum(b * p, axis=0, keepdims=True) for b, p in zip(beams, projected)]
            if step is None:
                misfit = [x - looked[d] for d, x in zip(ds, radial)]
                for d, x in zip(ds, misfit):
                    misfit0[d] = x
            else:
                misfit = [misfit0[d] - step * x for d, x in zip(ds, radial)]
            for x in misfit:
                cost = cost + x * x
            for u, (b, x) in enumerate(zip(beams, misfit)):
                held[u] = (b * x).astype(BF16)
            return cost

        def back(ds):
            return [jnp.dot(held[u], weights_of(d), preferred_element_type=F32) for u, d in enumerate(ds)]

        def send(ds, values, last):
            for d, x in zip(ds, values):
                out[d] = x.astype(BF16)
            for u, d in enumerate(ds):
                if last and u == group - 1:
                    dst[me] = out[me]
                else:
                    exchange_copy(stage, out, dst, d).start()

        def middle(q, cost):
            ds, ahead = members(q), members(q + 1)
            values = back(ds)
            projected = project(ahead)
            send(ds, values, False)
            return adjoints(ahead, projected, cost)

        first = members(0)
        cost = adjoints(first, project(first), jnp.zeros((1, 2 * LANES), F32))
        cost = lax.fori_loop(0, count - 1, middle, cost)
        final = members(count - 1)
        send(final, back(final), True)
        return 0.5 * jnp.sum(cost, axis=1, keepdims=True)

    def scatter(source, out, to_field):
        rows = jnp.swapaxes(source[...].astype(F32), 0, 1).astype(BF16)
        landed = jnp.concatenate(
            [jnp.concatenate([rows[3 * k + c] for c in range(3)], 1) for k in range(2)], 0)
        total = jnp.zeros((nz, LANES), F32)
        for h in range(ny // LANES):
            added = jnp.dot(place[h * half : (h + 1) * half], landed, preferred_element_type=F32)
            for c in range(3):
                lanes = slice(h * LANES, (h + 1) * LANES)
                v = added[:, c * LANES : (c + 1) * LANES].reshape(nx, nz, LANES) + push[c, :, :, lanes]
                out[c, 1 : nx + 1, :, lanes] = v
                total = total + jnp.sum(v * v, axis=0)
                if to_field:
                    field[h * half : (h + 1) * half, c * LANES : (c + 1) * LANES] = v.reshape(half, LANES).astype(BF16)
        return total_of(total)

    ahead = iota((1, LANES), 1) < LANES // 2

    def code_rows(q, carry):
        ds = [q * 8 + u for u in range(8)]
        counts = [count_ref[0, d] for d in ds]
        blocks = [[block_ref[0, 2 * d + k] for k in range(2)] for d in ds]
        rows = []
        for count, pair in zip(counts, blocks):
            codes = [lax.rem(b, ny // LANES) * half + lax.div(b, ny // LANES) for b in pair]
            codes = [jnp.where(k < count, c, -1) for k, c in enumerate(codes)]
            rows.append(jnp.where(ahead, codes[0], codes[1]))
        for d, row in zip(ds, rows):
            codes_out[d] = row
        return carry

    in1[:, 6:, :] = jnp.zeros((n, 2, LANES), BF16)
    load_blocks.wait()
    load_counts.wait()
    lax.fori_loop(0, n // 8, code_rows, 0)
    load_bg.wait()
    pack_edges(BACK, wind, 3, False)
    pl.semaphore_wait(barrier, n - 1)
    send_all(0, codes_out, codes_in)
    send_halos(BACK, wind)
    to_field(wind)

    load_beams.wait()
    load_looked.wait()
    beams32[...] = beams16[...].astype(F32)
    looked32[...] = looked16[...].astype(F32)
    zero = jnp.zeros((n, LANES), F32)
    rows = []
    for k in range(2):
        rows += [beams32[c, pl.ds(k, n, stride=2), :] for c in range(3)]
    rows += [zero, zero]
    out_row = jnp.swapaxes(jnp.stack(rows, 0), 0, 1)
    rays[:, :, :LANES] = out_row
    eight = iota((8, LANES), 0)

    def ray_rows(q, carry):
        ds = [q * 8 + u for u in range(8)]
        counts = [count_ref[0, d] for d in ds]
        values = [rays[d, :, :LANES] for d in ds]
        seen = [[looked32[pl.ds(2 * d + k, 1), :] for k in range(2)] for d in ds]
        for d, count, v, s in zip(ds, counts, values, seen):
            rays[d, :, :LANES] = jnp.where((eight < 3) & (count > 0), v, 0.0)
            rays[d, :, LANES:] = jnp.where((eight >= 3) & (count > 1), v, 0.0)
            looked[d] = jnp.concatenate([jnp.where(count > k, s[k], 0.0) for k in range(2)], 1)
        return carry

    lax.fori_loop(0, n // 8, ray_rows, 0)

    whole(0, codes_out, codes_in).wait_recv()
    codes = codes_in[...].reshape(n, LANES)
    turned = pltpu.roll(codes, LANES // 2, 1)
    front = iota((n, LANES), 1) < LANES // 2
    code = (jnp.where(front, codes, turned), jnp.where(front, turned, codes))
    for k in range(2):
        for j in range(pick.shape[1] // LANES):
            hit = code[k] == iota((n, LANES), 1) + j * LANES
            pick[k * n : (k + 1) * n, j * LANES : (j + 1) * LANES] = jnp.where(hit, 1.0, 0.0).astype(BF16)

    gather(out1, None)
    send_all(1, out1, in1)
    for k in range(2):
        across = jnp.transpose(code[k])
        for j in range(pick.shape[1] // LANES):
            hit = across == iota((LANES, n), 0) + j * LANES
            place[j * LANES : (j + 1) * LANES, k * n : (k + 1) * n] = jnp.where(hit, 1.0, 0.0).astype(BF16)
    await_halos(BACK, wind)
    spread_cost0 = 0.5 * DIVERGENCE_WEIGHT * total_of(divergence(BACK, wind, spread0))
    pack_edges(SPREAD0, spread0, 1, True)
    send_halos(SPREAD0, spread0, "one")
    load_interp.wait()
    whole(1, out1, in1).wait_recv()
    cost0 = observe(in1, out2, in2, 2, None) + spread_cost0
    await_halos(SPREAD0, spread0, "one")
    low, high = edges_in[SPREAD0, 0], edges_in[SPREAD0, 1]

    def push_plane(x, carry):
        values = pushes(SPREAD0, spread0, x, low, high)
        return [(push, (c, x), DIVERGENCE_WEIGHT * v) for c, v in enumerate(values)], carry

    over_planes(nx, push_plane, 0)
    whole(2, out2, in2).wait_recv()
    squares = scatter(in2, grad0, True)

    first = squares.astype(BF16)
    rest = squares - first.astype(F32)
    second = rest.astype(BF16)
    third = (rest - second.astype(F32)).astype(BF16)
    at = iota((1, LANES), 1)
    extra = jnp.where(at == 0, first.astype(F32), jnp.where(at == 1, second.astype(F32), jnp.where(at == 2, third.astype(F32), 0.0)))
    gather(out3, extra)
    pack_edges(GRAD0, grad0, 3, False)
    send_halos(GRAD0, grad0, "first")
    send_all(3, out3, in3)
    await_halos(GRAD0, grad0, "first")
    divergence(GRAD0, grad0, spread1)
    pack_edges(SPREAD1, spread1, 1, True)
    send_halos(SPREAD1, spread1, "one")
    whole(3, out3, in3).wait_recv()
    squares = jnp.sum(jnp.sum(in3[...].astype(F32), axis=0)[6:7], axis=1, keepdims=True)
    step0 = STEP_LENGTH / jnp.sqrt(squares / total_cells + EPSILON)
    cost1 = observe(in3, out4, in4, 4, step0)

    def wind_plane(x, carry):
        return [(wind, (c, x), wind[c, x] - step0 * grad0[c, x]) for c in range(3)], carry

    send_halos(REST0, grad0, "rest")
    await_halos(SPREAD1, spread1, "one")
    low1, high1 = edges_in[SPREAD1, 0], edges_in[SPREAD1, 1]

    def update_plane(x, carry):
        offsets, spreads = carry
        stores = []
        for c, v in enumerate(pushes(SPREAD1, spread1, x, low1, high1)):
            offset = -step0 * grad0[c, x + 1]
            offsets = offsets + offset * offset
            stores.append((push, (c, x), push[c, x] - step0 * (DIVERGENCE_WEIGHT * v) + BACKGROUND_WEIGHT * offset))
        spread = spread0[x + 1] - step0 * spread1[x + 1]
        return stores, (offsets, spreads + spread * spread)

    zero = jnp.zeros((nz, ny), F32)
    offsets, spreads = over_planes(nx, update_plane, (zero, zero))
    cost1 = cost1 + 0.5 * total_of(BACKGROUND_WEIGHT * offsets + DIVERGENCE_WEIGHT * spreads)
    whole(4, out4, in4).wait_recv()
    squares = scatter(in4, grad1, False)

    inner = pl.ds(1, nx)
    save_grad = pltpu.make_async_copy(grad1.at[:, inner], grad_out.at[:, inner], local_sems.at[7])
    summary = jnp.where(at == 0, squares, jnp.where(at == 1, cost0, jnp.where(at == 2, cost1, 0.0)))

    out5[...] = summary

    for_others(lambda d: pltpu.make_async_remote_copy(
        src_ref=out5, dst_ref=in5.at[me], send_sem=send_sems.at[5], recv_sem=recv_sems.at[5],
        device_id=d, device_id_type=LOGICAL).start())
    in5[me] = summary
    save_grad.start()
    pack_edges(GRAD1, grad1, 3, False)
    send_halos(GRAD1, grad1)
    await_halos(REST0, grad0, "rest")
    over_planes(nx + 2, wind_plane, 0)
    save_wind = pltpu.make_async_copy(wind, wind_out, local_sems.at[6])
    save_wind.start()
    for i in range(2):
        info[i] = edges_in[BACK, i] - step0 * edges_in[GRAD0, i]
    info[4] = jnp.zeros((nz, LANES), F32)
    await_halos(GRAD1, grad1)
    for i in range(2):
        info[2 + i] = edges_in[GRAD1, i]
    save_edges = [
        pltpu.make_async_copy(grad1.at[:, x], grad_out.at[:, x], local_sems.at[9 + i])
        for i, x in enumerate((0, nx + 1))]
    for copy in save_edges:
        copy.start()
    whole(5, in5, in5).wait_recv()
    sums = jnp.sum(in5[...], axis=0)
    squares = jnp.sum(jnp.where(at == 0, sums, 0.0), axis=1, keepdims=True)
    step1 = STEP_LENGTH / jnp.sqrt(squares / total_cells + EPSILON)
    info[4, 0:1, :] = jnp.where(at == 0, step1, sums / total_gates)
    save_info = pltpu.make_async_copy(info, info_out, local_sems.at[8])
    save_info.start()
    save_info.wait()
    for copy in save_edges:
        copy.wait()
    save_grad.wait()
    save_wind.wait()

    pairs = ((codes_out, codes_in), (out1, in1), (out2, in2), (out3, in3), (out4, in4), (in5, in5))
    for stage, (src, dst) in enumerate(pairs):
        whole(stage, src, dst).wait_send()


def strain_kernel(wind_hbm, grad_hbm, info_hbm, final_hbm, strain_hbm, trace_ref,
                  wind, grad, info, strain, wind_sems, grad_sems, info_sem, final_sems, strain_sems):
    nx, nz, ny = wind.shape[1] - 2, wind.shape[2], wind.shape[3]
    diff_y, diff_z = differences(nz, ny)
    load_info = pltpu.make_async_copy(info_hbm, info, info_sem)
    load_info.start()
    starts = list(range(0, nx + 2, 6))
    loads = []
    for i, start in enumerate(starts):
        span = pl.ds(start, min(6, nx + 2 - start))
        loads.append((
            pltpu.make_async_copy(wind_hbm.at[:, span], wind.at[:, span], wind_sems.at[i]),
            pltpu.make_async_copy(grad_hbm.at[:, span], grad.at[:, span], grad_sems.at[i])))
        for copy in loads[-1]:
            copy.start()
    load_info.wait()
    step = info[4, 0:1, 0:1]
    low, high = (info[i] - step * info[2 + i] for i in range(2))
    scalars = info[4, 0:1, :]
    at = iota((1, LANES), 1)
    for i in range(2):
        trace_ref[i] = jnp.sum(jnp.where(at == i + 1, scalars, 0.0))

    ready, saves = 0, []
    for j in range(nx // 2):
        while ready < len(starts) and starts[ready] <= 2 * j + 3:
            for copy in loads[ready]:
                copy.wait()
            for x in range(starts[ready], min(starts[ready] + 6, nx + 2)):
                new = [wind[c, x] - step * grad[c, x] for c in range(3)]
                for c in range(3):
                    wind[c, x] = new[c]
            ready += 1
        stores = []
        for x in (2 * j, 2 * j + 1):
            v = [wind[c, x + 1] for c in range(3)]
            dx = [0.5 * (wind[c, x + 2] - wind[c, x]) for c in range(3)]
            dy = [diff_y(v[c], low, high, x, c) for c in range(3)]
            dz = [diff_z(v[c]) for c in range(3)]
            values = (dx[0], dy[1], dz[2], 0.5 * (dy[0] + dx[1]), 0.5 * (dz[0] + dx[2]), 0.5 * (dz[1] + dy[2]))
            stores += [(c, x, value) for c, value in enumerate(values)]
        for c, x, value in stores:
            strain[c, x] = value
        pair = pl.ds(2 * j, 2)
        saves += [
            pltpu.make_async_copy(wind.at[:, pl.ds(2 * j + 1, 2)], final_hbm.at[:, pair], final_sems.at[j]),
            pltpu.make_async_copy(strain.at[:, pair], strain_hbm.at[:, pair], strain_sems.at[j])]
        for copy in saves[-2:]:
            copy.start()
    for copy in saves:
        copy.wait()


def shards(n_radar, n_tile, background, interp, beam, observed, cell_block, sweep_count):
    n = n_radar * n_tile
    _, nx, nz, ny = background.shape
    slots = interp.shape[0] // n
    gate = interp.shape[1]
    blocks = nx * nz * ny // gate
    total_cells = 3 * nx * nz * ny * n
    total_gates = interp.shape[0] * n * gate
    sizes = (n_radar, n_tile, total_cells, total_gates)
    torus = (2, n_tile // 4, 4)

    smem = pl.BlockSpec(memory_space=pltpu.SMEM)
    hbm = pl.BlockSpec(memory_space=pltpu.HBM)
    message = pltpu.VMEM((n, 8, LANES), BF16)
    row = pltpu.VMEM((n, 1, LANES), F32)
    code_row = pltpu.VMEM((n, 1, LANES), jnp.int32)
    padded = pltpu.VMEM((3, nx + 2, nz, ny), F32)
    single = pltpu.VMEM((nx + 2, nz, ny), F32)
    rays = jnp.transpose(beam, (1, 0, 2))
    groups = n // min(16, n // 2)
    wind, grad, info = pl.pallas_call(
        functools.partial(kernel, sizes, torus),
        name="wind_analysis",
        out_shape=(
            jax.ShapeDtypeStruct((3, nx + 2, nz, ny), F32),
            jax.ShapeDtypeStruct((3, nx + 2, nz, ny), F32),
            jax.ShapeDtypeStruct((5, nz, LANES), F32),
        ),
        in_specs=[hbm] * 6,
        out_specs=(hbm, hbm, hbm),
        scratch_shapes=[
            pltpu.VMEM(interp.shape, BF16),
            pltpu.VMEM(rays.shape, BF16),
            pltpu.VMEM(observed.shape, BF16),
            padded, padded, padded, single, single,
            pltpu.VMEM((3, nx, nz, ny), F32),
            pltpu.SMEM((1, n * slots), jnp.int32), pltpu.SMEM((1, n), jnp.int32),
            code_row, code_row, message, message, message, message, message, message, message, message, pltpu.VMEM((1, LANES), F32), row,
            pltpu.VMEM((5, nz, LANES), F32),
            pltpu.VMEM((slots * n, blocks), BF16),
            pltpu.VMEM((blocks, slots * n), BF16),
            pltpu.VMEM((blocks, 3 * LANES), BF16),
            pltpu.VMEM(rays.shape, F32),
            pltpu.VMEM(observed.shape, F32),
            pltpu.VMEM((n, 8, slots * gate), F32),
            pltpu.VMEM((n, 1, slots * gate), F32),
            pltpu.VMEM((n, 1, slots * gate), F32),
            pltpu.VMEM((n // groups, 8, slots * gate), BF16),
            pltpu.VMEM((5, 2, nz, LANES), F32),
            pltpu.VMEM((5, 2, nz, LANES), F32),
            pltpu.SemaphoreType.DMA((6,)),
            pltpu.SemaphoreType.DMA((6,)),
            pltpu.SemaphoreType.DMA((6, 4)),
            pltpu.SemaphoreType.DMA((6, 4)),
            pltpu.SemaphoreType.DMA((11,)),
        ],
        compiler_params=pltpu.CompilerParams(
            collective_id=0, has_side_effects=True, vmem_limit_bytes=60 * 2**20),
    )(cell_block.reshape(1, n * slots), sweep_count, background, interp, rays, observed)

    spans = len(range(0, nx + 2, 6))
    return pl.pallas_call(
        strain_kernel,
        name="strain",
        out_shape=(
            jax.ShapeDtypeStruct(background.shape, F32),
            jax.ShapeDtypeStruct((6, nx, nz, ny), F32),
            jax.ShapeDtypeStruct((2,), F32),
        ),
        in_specs=[hbm] * 3,
        out_specs=(hbm, hbm, smem),
        scratch_shapes=[
            padded, padded, pltpu.VMEM((5, nz, LANES), F32), pltpu.VMEM((6, nx, nz, ny), F32),
            pltpu.SemaphoreType.DMA((spans,)), pltpu.SemaphoreType.DMA((spans,)), pltpu.SemaphoreType.DMA,
            pltpu.SemaphoreType.DMA((nx // 2,)), pltpu.SemaphoreType.DMA((nx // 2,))],
        compiler_params=pltpu.CompilerParams(vmem_limit_bytes=60 * 2**20),
    )(wind, grad, info)


def solution(mesh):
    n_radar, n_tile = mesh.shape["radar"], mesh.shape["tile"]
    both = ("radar", "tile")
    in_specs = (
        P(None, "tile", None, "radar"), P(both, None, None), P(both, None, None),
        P(both, None), P(both), P(both, None))
    out_specs = (P(None, "tile", None, "radar"), P(None, "tile", None, "radar"), P())
    return jax.shard_map(
        functools.partial(shards, n_radar, n_tile), mesh=mesh, in_specs=in_specs, out_specs=out_specs, check_vma=False)
```
